128 devices in a mesh: chan: 2 (over core), row: 8 (over x_hi, y), col: 8 (over z, x_lo).
Axes of the slice: x: 4 (x_hi: 2, x_lo: 2; x = x_hi * 2 + x_lo), y: 4, z: 4, core: 2. Of those that a mesh axis runs over, the one named last changes fastest.
Arguments:
- pair_acts: bfloat16 [128, 1024, 1024], P('chan', 'row', 'col'), may hold values from -6 to 6
- residue_mask: int32 [1024], replicated, may hold values 0 or 1
- norm_in_gain: float32 [128], replicated, may hold values from 0.1 to 1.9
- w_proj: bfloat16 [5, 128, 128], P(None, 'chan'), may hold values from -0.5 to 0.5
- norm_out_gain: float32 [128], replicated, may hold values from 0.1 to 1.9
- w_out: bfloat16 [128, 128], P('chan'), may hold values from -0.5 to 0.5
Outputs:
- update: bfloat16 [128, 1024, 1024], P('chan', 'row', 'col')
The draws below stay inside these ranges and needn't reach their ends.
All inputs are finite; a program needn't handle non-finite values.
Results may differ from the reference program's by a relative error of at most 0.0082.
Values may be sent and summed in bfloat16 or wider, within the bound.
A program may use at most 128 MiB of HBM per device.

```python
import jax
import jax.numpy as jnp
from jax import lax

C = 128
N = 1024


def place_ends(drawn, key, smallest, largest):
    spot = [jax.random.randint(jax.random.fold_in(key, axis), (), 0, length) for axis, length in enumerate(drawn.shape)]
    longest = drawn.shape.index(max(drawn.shape))
    neighbour = spot[:longest] + [(spot[longest] + 1) % drawn.shape[longest]] + spot[longest + 1:]
    return drawn.at[tuple(spot)].set(smallest).at[tuple(neighbour)].set(largest)


def levels(stream_key, shape, cuts, smallest, largest):
    def one(axis_at, shards_of):
        heights = jax.random.uniform(jax.random.fold_in(jax.random.fold_in(stream_key, 6), axis_at), (shards_of,), jnp.float32, smallest / len(cuts), largest / len(cuts))
        return jnp.repeat(jnp.exp(heights), shape[axis_at] // shards_of).reshape((-1,) + (1,) * (len(shape) - axis_at - 1))

    level = one(*cuts[0])
    for cut in cuts[1:]:
        level = level * one(*cut)
    return level


def normal_values(key, extent, deviation, limit, split=(), dtype=jnp.bfloat16):
    entries = jax.random.normal(key, extent, jnp.float32) * deviation
    if len(split) > 0:
        entries = levels(key, extent, split, -0.22, 0.18) * entries
    return jnp.clip(entries, min=-limit, max=limit).astype(dtype)


def setup_inputs(seed: int = 0) -> dict:
    streams_of = jax.random.split(jax.random.key(seed), 7)
    pair_acts = normal_values(streams_of[0], (C, N, N), 1.0, 6.0, ((0, 2), (1, 8), (2, 8)))
    residue_mask = place_ends((jax.random.randint(streams_of[1], (N,), 0, 8) < 7).astype(jnp.int32), jax.random.fold_in(streams_of[1], 1), 0, 1)
    norm_in_gain = jnp.clip(1.0 + 0.18 * jax.random.normal(streams_of[2], (C,), jnp.float32), 0.1, 1.9)
    w_proj = normal_values(streams_of[3], (5, C, C), C ** -0.5, 0.5, ((1, 2),))
    norm_out_gain = jnp.clip(1.0 + 0.18 * jax.random.normal(streams_of[4], (C,), jnp.float32), 0.1, 1.9)
    w_out = normal_values(streams_of[5], (C, C), C ** -0.5, 0.5, ((0, 2),))
    return {"pair_acts": pair_acts, "residue_mask": residue_mask, "norm_in_gain": norm_in_gain, "w_proj": w_proj, "norm_out_gain": norm_out_gain, "w_out": w_out}


def normalize(values, gain_vector):
    center = lax.optimization_barrier(jnp.mean(values, axis=0, keepdims=True))
    spread = lax.optimization_barrier(jnp.mean(jnp.square(values - center), axis=0, keepdims=True))
    shaped = gain_vector.reshape((-1,) + (1,) * (values.ndim - 1))
    return (values - center) * lax.rsqrt(spread + 1e-05) * shaped

def reference(pair_acts, residue_mask, norm_in_gain, w_proj, norm_out_gain, w_out):
    channels = pair_acts.shape[0]
    length = pair_acts.shape[1]
    normed = normalize(pair_acts.astype(jnp.float32), norm_in_gain).astype(jnp.bfloat16)
    normed = normed.reshape(channels, length * length)

    def project(proj_index):
        return jnp.dot(w_proj[proj_index], normed, preferred_element_type=jnp.float32)
    weights_mask = residue_mask.astype(jnp.float32)
    pair_mask = (weights_mask[:, None] * weights_mask[None, :]).reshape(-1)
    left_side = (jax.nn.sigmoid(project(0)) * project(1) * pair_mask).astype(jnp.bfloat16)
    left_side = left_side.reshape(channels, length, length)
    right_side = (jax.nn.sigmoid(project(2)) * project(3) * pair_mask).astype(jnp.bfloat16)
    right_side = right_side.reshape(channels, length, length)

    def per_channel(operands):
        left_tile, right_tile = operands
        return jnp.dot(left_tile, right_tile.T, preferred_element_type=jnp.float32).astype(jnp.bfloat16)
    product = lax.map(per_channel, (left_side, right_side))
    normed_out = normalize(product.astype(jnp.float32), norm_out_gain).astype(jnp.bfloat16)
    normed_out = normed_out.reshape(channels, length * length)
    gate_values = jax.nn.sigmoid(project(4))
    mixed_out = jnp.dot(w_out, normed_out, preferred_element_type=jnp.float32)
    result = (gate_values * mixed_out).astype(jnp.bfloat16)
    return result.reshape(channels, length, length)
```

```python
import functools

import jax
import jax.numpy as jnp
from jax import lax
from jax.experimental import pallas as pl
from jax.experimental.pallas import tpu as pltpu
from jax.sharding import PartitionSpec as P

MESH = pl.DeviceIdType.MESH
BF16 = jnp.bfloat16
F32 = jnp.float32


def normalize(values, gain_vector):
    center = jnp.mean(values, axis=0, keepdims=True)
    spread = jnp.mean(jnp.square(values - center), axis=0, keepdims=True)
    shaped = gain_vector.reshape((-1,) + (1,) * (values.ndim - 1))
    return (values - center) * lax.rsqrt(spread + 1e-05) * shaped


def place():
    row, col = lax.axis_index("row"), lax.axis_index("col")
    return lax.axis_index("chan"), (row // 4) * 2 + col % 2, row % 4, col // 2


def device(h, x, y, z):
    return (h, (x // 2) * 4 + y, z * 2 + x % 2)


def offset(q, x, y, z):
    return (x + q // 16) % 4, (y + (q // 4) % 4) % 4, (z + q % 4) % 4


def exchange_kernel(left_ref, right_ref, out_ref, lbuf, rbuf, pbuf, lsend, lrecv, rsend, rrecv, psend, precv, own, xsend, xrecv):
    h, x, y, z = place()
    row, col = lax.axis_index("row"), lax.axis_index("col")
    me = (x * 4 + y) * 4 + z
    barrier = pltpu.get_barrier_semaphore()

    def greet(q, carry):
        pl.semaphore_signal(barrier, inc=1, device_id=device(h, *offset(q, x, y, z)), device_id_type=MESH)
        return carry

    lax.fori_loop(1, 64, greet, 0)
    pl.semaphore_signal(barrier, inc=1, device_id=device(1 - h, x, y, z), device_id_type=MESH)
    pl.semaphore_wait(barrier, 64)

    rows, cols = pl.ds(pl.multiple_of(row * 128, 128), 128), pl.ds(pl.multiple_of(col * 128, 128), 128)

    def scatter(source, target, send_sem, recv_sem):
        def send(o, carry):
            q = (o * 27) % 64
            tx, ty, tz = offset(q, x, y, z)
            pltpu.make_async_remote_copy(
                src_ref=source.at[(tx * 4 + ty) * 4 + tz],
                dst_ref=target.at[rows, cols],
                send_sem=send_sem,
                recv_sem=recv_sem,
                device_id=device(h, tx, ty, tz),
                device_id_type=MESH,
            ).start()
            return carry

        lax.fori_loop(1, 64, send, 0)

    scatter(right_ref, rbuf, rsend, rrecv)
    scatter(left_ref, lbuf, lsend, lrecv)
    copy_l = pltpu.make_async_copy(left_ref.at[me], lbuf.at[rows, cols], own.at[0])
    copy_r = pltpu.make_async_copy(right_ref.at[me], rbuf.at[rows, cols], own.at[1])
    copy_l.start()
    copy_r.start()
    copy_l.wait()
    copy_r.wait()

    def all_of(send_sem, recv_sem):
        return pltpu.make_async_remote_copy(
            src_ref=left_ref.at[pl.ds(0, 63)],
            dst_ref=pbuf.at[pl.ds(0, 63)],
            send_sem=send_sem,
            recv_sem=recv_sem,
            device_id=device(h, *offset(1, x, y, z)),
            device_id_type=MESH,
        )

    all_of(rsend, rrecv).wait()
    all_of(lsend, lrecv).wait()

    def product_rows(t, carry):
        r = (row + t) % 8
        for half in range(2):
            tile = lax.dot_general(
                lbuf[pl.ds(pl.multiple_of(r * 128, 128), 128), :],
                rbuf[half * 512 : half * 512 + 512, :],
                (((1,), (1,)), ((), ())),
                preferred_element_type=F32,
            ).astype(BF16)
            for c in range(4):
                pbuf[r * 8 + half * 4 + c] = tile[:, c * 128 : c * 128 + 128]

        def send(u, inner):
            c = (col + u) % 8

            @pl.when(jnp.logical_or(r != row, c != col))
            def _():
                pltpu.make_async_remote_copy(
                    src_ref=pbuf.at[r * 8 + c],
                    dst_ref=out_ref.at[h * 64 + me],
                    send_sem=psend,
                    recv_sem=precv,
                    device_id=(h, r, c),
                    device_id_type=MESH,
                ).start()

            return inner

        lax.fori_loop(0, 8, send, 0)
        return carry

    lax.fori_loop(0, 8, product_rows, 0)
    copy_p = pltpu.make_async_copy(pbuf.at[row * 8 + col], out_ref.at[h * 64 + me], own.at[0])
    copy_p.start()
    copy_p.wait()
    all_of(psend, precv).wait()
    swap = pltpu.make_async_remote_copy(
        src_ref=out_ref.at[pl.ds(h * 64, 64)],
        dst_ref=out_ref.at[pl.ds(h * 64, 64)],
        send_sem=xsend,
        recv_sem=xrecv,
        device_id=device(1 - h, x, y, z),
        device_id_type=MESH,
    )
    swap.start()
    swap.wait()


def exchange(left_side, right_side):
    vmem = pl.BlockSpec(memory_space=pltpu.VMEM)
    dma = pltpu.SemaphoreType.DMA
    return pl.pallas_call(
        exchange_kernel,
        out_shape=jax.ShapeDtypeStruct((128, 128, 128), BF16),
        in_specs=[vmem, vmem],
        out_specs=vmem,
        scratch_shapes=[
            pltpu.VMEM((1024, 1024), BF16),
            pltpu.VMEM((1024, 1024), BF16),
            pltpu.VMEM((64, 128, 128), BF16),
            dma,
            dma,
            dma,
            dma,
            dma,
            dma,
            dma((2,)),
            dma,
            dma,
        ],
        compiler_params=pltpu.CompilerParams(collective_id=1, has_side_effects=True, vmem_limit_bytes=48 << 20),
        name="triangle",
    )(left_side, right_side)


def body(pair_acts, residue_mask, norm_in_gain, w_proj, norm_out_gain, w_out):
    own_channels = pair_acts.shape[0]
    tile_size = pair_acts.shape[1]
    whole_pair = lax.all_gather(pair_acts, "chan", axis=0, tiled=True)
    total_channels = whole_pair.shape[0]
    normed = normalize(whole_pair.astype(F32), norm_in_gain).astype(BF16)
    normed = normed.reshape(total_channels, tile_size * tile_size)

    def project(proj_index):
        return jnp.dot(w_proj[proj_index], normed, preferred_element_type=F32)

    row_place = lax.axis_index("row")
    col_place = lax.axis_index("col")
    row_mask = lax.dynamic_slice_in_dim(residue_mask, row_place * tile_size, tile_size).astype(F32)
    col_mask = lax.dynamic_slice_in_dim(residue_mask, col_place * tile_size, tile_size).astype(F32)
    pair_mask = (row_mask[:, None] * col_mask[None, :]).reshape(-1)
    left_side = (jax.nn.sigmoid(project(0)) * project(1) * pair_mask).astype(BF16)
    left_side = left_side.reshape(own_channels, tile_size, tile_size)
    right_side = (jax.nn.sigmoid(project(2)) * project(3) * pair_mask).astype(BF16)
    right_side = right_side.reshape(own_channels, tile_size, tile_size)
    full_product = exchange(left_side, right_side)
    normed_out = normalize(full_product.astype(F32), norm_out_gain).astype(BF16)
    normed_out = normed_out.reshape(total_channels, tile_size * tile_size)
    mixed_out = jnp.dot(w_out, normed_out, preferred_element_type=F32)
    result = (jax.nn.sigmoid(project(4)) * mixed_out).astype(BF16)
    return result.reshape(own_channels, tile_size, tile_size)


def solution(mesh):
    return jax.shard_map(
        body,
        mesh=mesh,
        in_specs=(P("chan", "row", "col"), P(), P(), P(None, "chan", None), P(), P("chan", None)),
        out_specs=P("chan", "row", "col"),
        check_vma=False,
    )
```

```python
import functools

import jax
import jax.numpy as jnp
from jax import lax
from jax.experimental import pallas as pl
from jax.experimental.pallas import tpu as pltpu
from jax.sharding import PartitionSpec as P

MESH = pl.DeviceIdType.MESH
BF16 = jnp.bfloat16
F32 = jnp.float32
CHANNELS = 128
OWN = 64
TILE = 128
CHUNKS = 4
STEP = TILE // CHUNKS
GROUP = 16
BLOCK = 8


def place():
    row, col = lax.axis_index("row"), lax.axis_index("col")
    return lax.axis_index("chan"), (row // 4) * 2 + col % 2, row % 4, col // 2


def device(h, x, y, z):
    return (h, (x // 2) * 4 + y, z * 2 + x % 2)


def offset(q, x, y, z):
    return (x + q // 16) % 4, (y + (q // 4) % 4) % 4, (z + q % 4) % 4


def aligned(start, size):
    return pl.ds(pl.multiple_of(start, size), size)


def sigmoid(value):
    return 0.5 * jnp.tanh(0.5 * value) + 0.5


def layer_norm(source, rows, gain, target):
    def total(b, acc):
        return acc + jnp.sum(source[pl.ds(b * BLOCK, BLOCK), rows, :].astype(F32), axis=0)

    zero = jnp.zeros((GROUP, TILE), F32)
    center = lax.fori_loop(0, CHANNELS // BLOCK, total, zero) * (1.0 / CHANNELS)

    def squares(b, acc):
        shifted = source[pl.ds(b * BLOCK, BLOCK), rows, :].astype(F32) - center[None]
        return acc + jnp.sum(shifted * shifted, axis=0)

    spread = lax.fori_loop(0, CHANNELS // BLOCK, squares, zero) * (1.0 / CHANNELS)
    scale = lax.rsqrt(spread + 1e-05)

    def write(b, carry):
        for u in range(BLOCK):
            c = b * BLOCK + u
            target[aligned(c * GROUP, GROUP), :] = (source[c, rows, :].astype(F32) - center) * scale * gain[c]
        return carry

    lax.fori_loop(0, CHANNELS // BLOCK, write, 0)


def two_rows(source, p):
    first = source[pl.ds(2 * p, CHANNELS, stride=GROUP), :].astype(BF16)
    second = source[pl.ds(2 * p + 1, CHANNELS, stride=GROUP), :].astype(BF16)
    return jnp.concatenate([first, second], axis=1)


def put_rows(target, p, value):
    target[pl.ds(2 * p, OWN, stride=GROUP), :] = value[:, :TILE]
    target[pl.ds(2 * p + 1, OWN, stride=GROUP), :] = value[:, TILE:]


def pack(source, target, rows):
    def step(b, carry):
        block = source[aligned(b * BLOCK * GROUP, BLOCK * GROUP), :]
        target[pl.ds(b * BLOCK, BLOCK), rows, :] = block.reshape(BLOCK, GROUP, TILE).astype(BF16)
        return carry

    lax.fori_loop(0, OWN // BLOCK, step, 0)


def kernel(
    pair, mask_s, gain_in, gain_out, mask_v, w_in, w_out, out,
    whole, normed, stage_a, stage_b, left, right, gate, lbuf, rbuf, rturn, pbuf, prod, result,
    own_x, xsend, xrecv, rsend, rrecv, lsend, lrecv, psend, precv, qsend, qrecv, own, done,
):
    h, x, y, z = place()
    row, col = lax.axis_index("row"), lax.axis_index("col")
    me = (x * 4 + y) * 4 + z
    partner = device(1 - h, x, y, z)
    mine = pl.ds(h * OWN, OWN)
    cols = aligned(col * TILE, TILE)

    def rows_of(s):
        return aligned(s * STEP, STEP)

    def load(s):
        return pltpu.make_async_copy(pair.at[:, rows_of(s), :], whole.at[mine, rows_of(s), :], own_x.at[s])

    def swap(s):
        return pltpu.make_async_remote_copy(
            src_ref=pair.at[:, rows_of(s), :],
            dst_ref=whole.at[mine, rows_of(s), :],
            send_sem=xsend.at[s],
            recv_sem=xrecv.at[s],
            device_id=partner,
            device_id_type=MESH,
        )

    for s in range(CHUNKS):
        load(s).start()
    barrier = pltpu.get_barrier_semaphore()
    pl.semaphore_signal(barrier, inc=1, device_id=partner, device_id_type=MESH)

    def greet(q, carry):
        pl.semaphore_signal(barrier, inc=1, device_id=device(h, *offset(q, x, y, z)), device_id_type=MESH)
        return carry

    lax.fori_loop(1, 64, greet, 0)
    pl.semaphore_wait(barrier, 64)
    for s in range(CHUNKS):
        swap(s).start()

    def scatter(source, s, target, send_sem, recv_sem, own_sem):
        def send(o, carry):
            q = (o * 27) % 64
            tx, ty, tz = offset(q, x, y, z)
            pltpu.make_async_remote_copy(
                src_ref=source.at[(tx * 4 + ty) * 4 + tz, rows_of(s), :],
                dst_ref=target,
                send_sem=send_sem,
                recv_sem=recv_sem,
                device_id=device(h, tx, ty, tz),
                device_id_type=MESH,
            ).start()
            return carry

        lax.fori_loop(1, 64, send, 0)
        pltpu.make_async_copy(source.at[me, rows_of(s), :], target, own_sem).start()

    def others(send_sem, recv_sem, size):
        return pltpu.make_async_remote_copy(
            src_ref=left.at[pl.ds(0, 63), pl.ds(0, size), :],
            dst_ref=right.at[pl.ds(0, 63), pl.ds(0, size), :],
            send_sem=send_sem,
            recv_sem=recv_sem,
            device_id=partner,
            device_id_type=MESH,
        )

    def right_target(s):
        return rbuf.at[aligned(row * TILE + s * STEP, STEP), cols]

    def left_target(s):
        return lbuf.at[s, aligned(row * STEP, STEP), cols]

    col_mask = mask_v[pl.ds(col, 1), :].astype(F32)

    def front(s, carry):
        load(s).wait()
        swap(s).wait()

        def group(g, inner):
            first = s * STEP + g * GROUP
            rows = aligned(first, GROUP)
            layer_norm(whole, rows, gain_in, normed)
            for p in range(GROUP // 2):
                i = first + 2 * p
                proj = jnp.dot(w_in[...], two_rows(normed, p), preferred_element_type=F32)
                mask = jnp.concatenate(
                    [col_mask * mask_s[row * TILE + i + e].astype(F32) for e in range(2)], axis=1
                )
                put_rows(stage_a, p, sigmoid(proj[0:64]) * proj[64:128] * mask)
                put_rows(stage_b, p, sigmoid(proj[128:192]) * proj[192:256] * mask)
                opened = sigmoid(proj[256:320])
                gate[i] = opened[:, :TILE]
                gate[i + 1] = opened[:, TILE:]
            pack(stage_b, right, rows)
            pack(stage_a, left, rows)
            return inner

        lax.fori_loop(0, STEP // GROUP, group, 0)
        scatter(right, s, right_target(s), rsend, rrecv, own.at[0, s])
        return carry

    lax.fori_loop(0, CHUNKS, front, 0)

    def send_left(s, carry):
        scatter(left, s, left_target(s), lsend, lrecv.at[s], own.at[1, s])
        return carry

    lax.fori_loop(0, CHUNKS, send_left, 0)

    for s in range(CHUNKS):
        pltpu.make_async_copy(right.at[me, rows_of(s), :], right_target(s), own.at[0, s]).wait()
    others(rsend, rrecv, TILE).wait_recv()
    for b in range(8):
        rturn[:, b * TILE : b * TILE + TILE] = rbuf[b * TILE : b * TILE + TILE, :].T

    def middle(s, carry):
        pltpu.make_async_copy(left.at[me, rows_of(s), :], left_target(s), own.at[1, s]).wait()
        others(lsend, lrecv.at[s], STEP).wait_recv()
        for half in range(2):
            tile = jnp.dot(
                lbuf[s], rturn[:, half * 512 : half * 512 + 512], preferred_element_type=F32
            ).astype(BF16)
            for r in range(8):
                for c in range(4):
                    pbuf[s, r * 8 + half * 4 + c] = tile[r * STEP : r * STEP + STEP, c * TILE : c * TILE + TILE]

        def send(o, inner):
            q = (o * 27) % 64
            tx, ty, tz = offset(q, x, y, z)
            _, r, c = device(h, tx, ty, tz)
            pltpu.make_async_remote_copy(
                src_ref=pbuf.at[s, r * 8 + c],
                dst_ref=prod.at[h * OWN + me, rows_of(s), :],
                send_sem=psend,
                recv_sem=precv.at[s],
                device_id=(h, r, c),
                device_id_type=MESH,
            ).start()
            return inner

        lax.fori_loop(1, 64, send, 0)
        own_product(s).start()
        return carry

    def own_product(s):
        return pltpu.make_async_copy(
            pbuf.at[s, row * 8 + col], prod.at[h * OWN + me, rows_of(s), :], own.at[2, s]
        )

    def swap_product(s):
        return pltpu.make_async_remote_copy(
            src_ref=prod.at[mine, rows_of(s), :],
            dst_ref=prod.at[mine, rows_of(s), :],
            send_sem=qsend.at[s],
            recv_sem=qrecv.at[s],
            device_id=partner,
            device_id_type=MESH,
        )

    def write_out(s):
        return pltpu.make_async_copy(result.at[:, rows_of(s), :], out.at[:, rows_of(s), :], done.at[s])

    lax.fori_loop(0, CHUNKS, middle, 0)

    def back(s, carry):
        @pl.when(s < CHUNKS)
        def _():
            own_product(s).wait()
            others(psend, precv.at[s], STEP).wait_recv()
            swap_product(s).start()

        @pl.when(s > 0)
        def _():
            swap_product(s - 1).wait()

            def group(g, inner):
                first = (s - 1) * STEP + g * GROUP
                rows = aligned(first, GROUP)
                layer_norm(prod, rows, gain_out, normed)
                for p in range(GROUP // 2):
                    i = first + 2 * p
                    mixed = jnp.dot(w_out[...], two_rows(normed, p), preferred_element_type=F32)
                    put_rows(stage_a, p, mixed * jnp.concatenate([gate[i], gate[i + 1]], axis=1))
                pack(stage_a, result, rows)
                return inner

            lax.fori_loop(0, STEP // GROUP, group, 0)
            write_out(s - 1).start()

        return carry

    lax.fori_loop(0, CHUNKS + 1, back, 0)
    others(rsend, rrecv, TILE).wait_send()
    others(lsend, rrecv, TILE).wait_send()
    others(psend, rrecv, TILE).wait_send()
    for s in range(CHUNKS):
        write_out(s).wait()


def body(pair_acts, residue_mask, norm_in_gain, w_proj, norm_out_gain, w_out):
    vmem = pl.BlockSpec(memory_space=pltpu.VMEM)
    smem = pl.BlockSpec(memory_space=pltpu.SMEM)
    hbm = pl.BlockSpec(memory_space=pl.ANY)
    dma = pltpu.SemaphoreType.DMA
    return pl.pallas_call(
        kernel,
        out_shape=jax.ShapeDtypeStruct((OWN, TILE, TILE), BF16),
        in_specs=[hbm, smem, smem, smem, vmem, vmem, vmem],
        out_specs=hbm,
        scratch_shapes=[
            pltpu.VMEM((CHANNELS, TILE, TILE), BF16),
            pltpu.VMEM((CHANNELS * GROUP, TILE), F32),
            pltpu.VMEM((OWN * GROUP, TILE), F32),
            pltpu.VMEM((OWN * GROUP, TILE), F32),
            pltpu.VMEM((OWN, TILE, TILE), BF16),
            pltpu.VMEM((OWN, TILE, TILE), BF16),
            pltpu.VMEM((TILE, OWN, TILE), F32),
            pltpu.VMEM((CHUNKS, 8 * STEP, 8 * TILE), BF16),
            pltpu.VMEM((8 * TILE, 8 * TILE), BF16),
            pltpu.VMEM((8 * TILE, 8 * TILE), BF16),
            pltpu.VMEM((CHUNKS, 64, STEP, TILE), BF16),
            pltpu.VMEM((CHANNELS, TILE, TILE), BF16),
            pltpu.VMEM((OWN, TILE, TILE), BF16),
            dma((CHUNKS,)),
            dma((CHUNKS,)),
            dma((CHUNKS,)),
            dma,
            dma,
            dma,
            dma((CHUNKS,)),
            dma,
            dma((CHUNKS,)),
            dma((CHUNKS,)),
            dma((CHUNKS,)),
            dma((3, CHUNKS)),
            dma((CHUNKS,)),
        ],
        compiler_params=pltpu.CompilerParams(
            collective_id=1, has_side_effects=True, vmem_limit_bytes=56 << 20
        ),
        name="triangle",
    )(
        pair_acts,
        residue_mask,
        norm_in_gain,
        norm_out_gain,
        residue_mask.reshape(8, TILE),
        w_proj.reshape(5 * OWN, CHANNELS),
        w_out,
    )


def solution(mesh):
    return jax.shard_map(
        body,
        mesh=mesh,
        in_specs=(P("chan", "row", "col"), P(), P(), P(None, "chan", None), P(), P("chan", None)),
        out_specs=P("chan", "row", "col"),
        check_vma=False,
    )
```

```python
import jax
import jax.numpy as jnp
from jax import lax
from jax.experimental import pallas as pl
from jax.experimental.pallas import tpu as pltpu
from jax.sharding import PartitionSpec as P

LOGICAL = pl.DeviceIdType.LOGICAL
BF16 = jnp.bfloat16
F32 = jnp.float32
CHANNELS = 128
OWN = 64
TILE = 128
GROUP = 16
BLOCK = 8
X_CHUNKS = ((0, 16), (16, 48), (64, 64))
R_CHUNKS = ((0, 16), (16, 32), (48, 32), (80, 48))
L_CHUNKS = ((0, 32), (32, 32), (64, 32), (96, 16), (112, 16))
INNER = [(1, 2), (2, 1), (3, 3), (0, 1), (1, 0), (3, 2), (2, 3), (0, 2), (2, 0), (1, 1), (3, 1), (1, 3), (0, 3), (3, 0), (2, 2), (0, 0)]


def place():
    row, col = lax.axis_index("row"), lax.axis_index("col")
    return lax.axis_index("chan"), (row // 4) * 2 + col % 2, row % 4, col // 2


def peers(visit):
    _, x, y, z = place()
    along_y = [((y + d) % 4) * 8 for d in range(4)]
    along_z = [((z + d) % 4) * 2 for d in range(4)]

    def step(k, carry):
        d = (k + 1) % 4
        t = (x + d) % 4
        base = (t // 2) * 32 + t % 2
        for dy, dz in INNER[:15]:
            visit(base + along_y[dy] + along_z[dz])

        @pl.when(d != 0)
        def _():
            visit(base + along_y[0] + along_z[0])

        return carry

    lax.fori_loop(0, 4, step, 0)


def aligned(start, size):
    return pl.ds(pl.multiple_of(start, GROUP), size)


def sigmoid(value):
    return 0.5 * jnp.tanh(0.5 * value) + 0.5


def layer_norm(source, rows, gain, target):
    def part(b):
        return source[pl.ds(b * BLOCK, BLOCK), rows, :].astype(F32)

    zero = jnp.zeros((BLOCK, GROUP, TILE), F32)
    steps = CHANNELS // BLOCK

    def total(b, acc):
        return acc + part(b)

    center = jnp.sum(lax.fori_loop(0, steps, total, zero, unroll=2), axis=0) * (1.0 / CHANNELS)

    def squares(b, acc):
        shifted = part(b) - center[None]
        return acc + shifted * shifted

    spread = jnp.sum(lax.fori_loop(0, steps, squares, zero, unroll=2), axis=0) * (1.0 / CHANNELS)
    scale = lax.rsqrt(spread + 1e-05)

    def write(b, carry):
        for u in range(BLOCK):
            c = b * BLOCK + u
            target[pl.ds(pl.multiple_of(c * GROUP, GROUP), GROUP), :] = (
                (source[c, rows, :].astype(F32) - center) * scale * gain[c]
            )
        return carry

    lax.fori_loop(0, steps, write, 0, unroll=2)


def two_rows(source, p):
    first = source[pl.ds(2 * p, CHANNELS, stride=GROUP), :].astype(BF16)
    second = source[pl.ds(2 * p + 1, CHANNELS, stride=GROUP), :].astype(BF16)
    return jnp.concatenate([first, second], axis=1)


def put_rows(target, p, value):
    target[pl.ds(2 * p, OWN, stride=GROUP), :] = value[:, :TILE]
    target[pl.ds(2 * p + 1, OWN, stride=GROUP), :] = value[:, TILE:]


def pack(source, target, rows):
    def step(b, carry):
        block = source[pl.ds(pl.multiple_of(b * BLOCK * GROUP, GROUP), BLOCK * GROUP), :]
        target[pl.ds(b * BLOCK, BLOCK), rows, :] = block.reshape(BLOCK, GROUP, TILE).astype(BF16)
        return carry

    lax.fori_loop(0, OWN // BLOCK, step, 0, unroll=2)


def kernel(
    pair, mask_s, gain_in, gain_out, mask_v, w_in, w_out, out,
    whole, normed, stage_a, stage_b, left, right, gate, lbuf, rbuf, rturn, pbuf, prod,
    own_x, xsend, xrecv, rsend, rrecv, lsend, lrecv, psend, precv, qsend, qrecv, own,
):
    h = lax.axis_index("chan")
    row, col = lax.axis_index("row"), lax.axis_index("col")
    me = row * 8 + col
    home = h * OWN
    partner = (1 - h) * OWN + me
    mine = pl.ds(home, OWN)
    cols = pl.ds(pl.multiple_of(col * TILE, TILE), TILE)

    def load(k):
        rows = pl.ds(*X_CHUNKS[k])
        return pltpu.make_async_copy(pair.at[:, rows, :], whole.at[mine, rows, :], own_x.at[k])

    def swap(k):
        rows = pl.ds(*X_CHUNKS[k])
        return pltpu.make_async_remote_copy(
            src_ref=pair.at[:, rows, :],
            dst_ref=whole.at[mine, rows, :],
            send_sem=xsend.at[k],
            recv_sem=xrecv.at[k],
            device_id=partner,
            device_id_type=LOGICAL,
        )

    for k in range(len(X_CHUNKS)):
        load(k).start()
    barrier = pltpu.get_barrier_semaphore()
    pl.semaphore_signal(barrier, inc=1, device_id=partner, device_id_type=LOGICAL)
    peers(lambda t: pl.semaphore_signal(barrier, inc=1, device_id=home + t, device_id_type=LOGICAL))
    pl.semaphore_wait(barrier, 64)
    for k in range(len(X_CHUNKS)):
        swap(k).start()

    def scatter(source, rows, target, send_sem, recv_sem, own_sem):
        def send(t):
            pltpu.make_async_remote_copy(
                src_ref=source.at[t, rows, :],
                dst_ref=target,
                send_sem=send_sem,
                recv_sem=recv_sem,
                device_id=home + t,
                device_id_type=LOGICAL,
            ).start()

        peers(send)
        pltpu.make_async_copy(source.at[me, rows, :], target, own_sem).start()

    def others(send_sem, recv_sem, size):
        return pltpu.make_async_remote_copy(
            src_ref=left.at[pl.ds(0, 63), pl.ds(0, size), :],
            dst_ref=right.at[pl.ds(0, 63), pl.ds(0, size), :],
            send_sem=send_sem,
            recv_sem=recv_sem,
            device_id=partner,
            device_id_type=LOGICAL,
        )

    def right_target(first, size):
        return rbuf.at[aligned(row * TILE + first, size), cols]

    def left_target(first, size):
        return lbuf.at[aligned(first * 8 + row * size, size), cols]

    col_mask = mask_v[pl.ds(col, 1), :].astype(F32)

    def front(g, carry):
        for k, (start, _) in enumerate(X_CHUNKS):

            @pl.when(g * GROUP == start)
            def _():
                load(k).wait()
                swap(k).wait()

        first = g * GROUP
        rows = aligned(first, GROUP)
        layer_norm(whole, rows, gain_in, normed)
        for p in range(GROUP // 2):
            i = first + 2 * p
            proj = jnp.dot(w_in[...], two_rows(normed, p), preferred_element_type=F32)
            mask = jnp.concatenate([col_mask * mask_s[row * TILE + i + e].astype(F32) for e in range(2)], axis=1)
            put_rows(stage_a, p, sigmoid(proj[0:64]) * proj[64:128] * mask)
            put_rows(stage_b, p, sigmoid(proj[128:192]) * proj[192:256] * mask)
            opened = sigmoid(proj[256:320])
            gate[i] = opened[:, :TILE]
            gate[i + 1] = opened[:, TILE:]
        pack(stage_b, right, rows)
        pack(stage_a, left, rows)
        for k, (start, size) in enumerate(R_CHUNKS):

            @pl.when(first + GROUP == start + size)
            def _():
                scatter(right, pl.ds(start, size), right_target(start, size), rsend, rrecv, own.at[0, k])

        return carry

    lax.fori_loop(0, TILE // GROUP, front, 0)
    for k, (start, size) in enumerate(L_CHUNKS):
        scatter(left, pl.ds(start, size), left_target(start, size), lsend, lrecv.at[k], own.at[1, k])

    for k, (start, size) in enumerate(R_CHUNKS):
        pltpu.make_async_copy(right.at[me, pl.ds(start, size), :], right_target(start, size), own.at[0, k]).wait()
    others(rsend, rrecv, TILE).wait_recv()
    for b in range(8):
        rturn[:, b * TILE : b * TILE + TILE] = rbuf[b * TILE : b * TILE + TILE, :].T

    def product_slice(k, t):
        start, size = L_CHUNKS[k]
        return pbuf.at[t, pl.ds(start, size), :]

    def own_product(k):
        rows = pl.ds(*L_CHUNKS[k])
        return pltpu.make_async_copy(product_slice(k, me), prod.at[home + me, rows, :], own.at[2, k])

    def swap_product(k):
        rows = pl.ds(*L_CHUNKS[k])
        return pltpu.make_async_remote_copy(
            src_ref=prod.at[mine, rows, :],
            dst_ref=prod.at[mine, rows, :],
            send_sem=qsend.at[k],
            recv_sem=qrecv.at[k],
            device_id=partner,
            device_id_type=LOGICAL,
        )

    for k, (start, size) in enumerate(L_CHUNKS):
        pltpu.make_async_copy(left.at[me, pl.ds(start, size), :], left_target(start, size), own.at[1, k]).wait()
        others(lsend, lrecv.at[k], size).wait_recv()
        for half in range(2):
            tile = jnp.dot(
                lbuf[start * 8 : (start + size) * 8, :],
                rturn[:, half * 512 : half * 512 + 512],
                preferred_element_type=F32,
            ).astype(BF16)
            for r in range(8):
                for c in range(4):
                    pbuf[r * 8 + half * 4 + c, start : start + size, :] = tile[
                        r * size : r * size + size, c * TILE : c * TILE + TILE
                    ]
        rows = pl.ds(start, size)

        def send(t):
            pltpu.make_async_remote_copy(
                src_ref=product_slice(k, t),
                dst_ref=prod.at[home + me, rows, :],
                send_sem=psend,
                recv_sem=precv.at[k],
                device_id=home + t,
                device_id_type=LOGICAL,
            ).start()

        peers(send)
        own_product(k).start()

    def finish(first):
        rows = aligned(first, GROUP)
        layer_norm(prod, rows, gain_out, normed)
        for p in range(GROUP // 2):
            i = first + 2 * p
            mixed = jnp.dot(w_out[...], two_rows(normed, p), preferred_element_type=F32)
            put_rows(stage_a, p, mixed * jnp.concatenate([gate[i], gate[i + 1]], axis=1))
        pack(stage_a, out, rows)

    for k in range(len(L_CHUNKS) + 1):
        if k < len(L_CHUNKS):
            own_product(k).wait()
            others(psend, precv.at[k], L_CHUNKS[k][1]).wait_recv()
            swap_product(k).start()
        if k > 0:
            swap_product(k - 1).wait()
            start, size = L_CHUNKS[k - 1]

            def group(g, carry):
                finish(start + g * GROUP)
                return carry

            lax.fori_loop(0, size // GROUP, group, 0)
    others(rsend, rrecv, TILE).wait_send()
    others(lsend, rrecv, TILE).wait_send()
    others(psend, rrecv, TILE).wait_send()


def body(pair_acts, residue_mask, norm_in_gain, w_proj, norm_out_gain, w_out):
    vmem = pl.BlockSpec(memory_space=pltpu.VMEM)
    smem = pl.BlockSpec(memory_space=pltpu.SMEM)
    dma = pltpu.SemaphoreType.DMA
    parts = len(L_CHUNKS)
    return pl.pallas_call(
        kernel,
        out_shape=pltpu.VMEM((OWN, TILE, TILE), BF16),
        in_specs=[pl.BlockSpec(memory_space=pl.ANY), smem, smem, smem, vmem, vmem, vmem],
        out_specs=vmem,
        scratch_shapes=[
            pltpu.VMEM((CHANNELS, TILE, TILE), BF16),
            pltpu.VMEM((CHANNELS * GROUP, TILE), F32),
            pltpu.VMEM((OWN * GROUP, TILE), F32),
            pltpu.VMEM((OWN * GROUP, TILE), F32),
            pltpu.VMEM((OWN, TILE, TILE), BF16),
            pltpu.VMEM((OWN, TILE, TILE), BF16),
            pltpu.VMEM((TILE, OWN, TILE), F32),
            pltpu.VMEM((8 * TILE, 8 * TILE), BF16),
            pltpu.VMEM((8 * TILE, 8 * TILE), BF16),
            pltpu.VMEM((8 * TILE, 8 * TILE), BF16),
            pltpu.VMEM((64, TILE, TILE), BF16),
            pltpu.VMEM((CHANNELS, TILE, TILE), BF16),
            dma((len(X_CHUNKS),)),
            dma((len(X_CHUNKS),)),
            dma((len(X_CHUNKS),)),
            dma,
            dma,
            dma,
            dma((parts,)),
            dma,
            dma((parts,)),
            dma((parts,)),
            dma((parts,)),
            dma((3, parts)),
        ],
        compiler_params=pltpu.CompilerParams(collective_id=1, has_side_effects=True, vmem_limit_bytes=56 << 20),
        name="triangle",
    )(
        pair_acts,
        residue_mask,
        norm_in_gain,
        norm_out_gain,
        residue_mask.reshape(8, TILE),
        w_proj.reshape(5 * OWN, CHANNELS),
        w_out,
    )


def solution(mesh):
    return jax.shard_map(
        body,
        mesh=mesh,
        in_specs=(P("chan", "row", "col"), P(), P(), P(None, "chan", None), P(), P("chan", None)),
        out_specs=P("chan", "row", "col"),
        check_vma=False,
    )
```

```python
import jax
import jax.numpy as jnp
from jax import lax
from jax.experimental import pallas as pl
from jax.experimental.pallas import tpu as pltpu
from jax.sharding import PartitionSpec as P

LOGICAL = pl.DeviceIdType.LOGICAL
BF16 = jnp.bfloat16
F32 = jnp.float32
CHANNELS = 128
OWN = 64
TILE = 128
GROUP = 16
BLOCK = 8
X_CHUNKS = ((0, 16), (16, 48), (64, 64))
R_CHUNKS = ((0, 16), (16, 16), (32, 32), (64, 32), (96, 32))
L_CHUNKS = ((0, 32), (32, 32), (64, 32), (96, 16), (112, 16))
INNER = [(1, 2), (2, 1), (3, 3), (0, 1), (1, 0), (3, 2), (2, 3), (0, 2), (2, 0), (1, 1), (3, 1), (1, 3), (0, 3), (3, 0), (2, 2), (0, 0)]


def place():
    row, col = lax.axis_index("row"), lax.axis_index("col")
    return lax.axis_index("chan"), (row // 4) * 2 + col % 2, row % 4, col // 2


def peers(visit):
    _, x, y, z = place()
    along_y = [((y + d) % 4) * 8 for d in range(4)]
    along_z = [((z + d) % 4) * 2 for d in range(4)]

    def step(k, carry):
        d = (k + 1) % 4
        t = (x + d) % 4
        base = (t // 2) * 32 + t % 2
        for dy, dz in INNER[:15]:
            visit(base + along_y[dy] + along_z[dz])

        @pl.when(d != 0)
        def _():
            visit(base + along_y[0] + along_z[0])

        return carry

    lax.fori_loop(0, 4, step, 0)


def greet(visit):
    _, x, y, z = place()
    along_x = [(((x + d) % 4) // 2) * 32 + (x + d) % 2 for d in range(4)]
    along_y = [((y + d) % 4) * 8 for d in range(4)]
    along_z = [((z + d) % 4) * 2 for d in range(4)]
    offsets = [(a, b, c) for a in range(4) for b in range(4) for c in range(4)][1:]
    for a, b, c in sorted(offsets, key=lambda o: -sum(min(d, 4 - d) for d in o)):
        visit(along_x[a] + along_y[b] + along_z[c])


def aligned(start, size):
    return pl.ds(pl.multiple_of(start, GROUP), size)


def sigmoid(value):
    return 0.5 * jnp.tanh(0.5 * value) + 0.5


def layer_norm(source, rows, gain, target):
    def part(b):
        return source[pl.ds(b * BLOCK, BLOCK), rows, :].astype(F32)

    zero = jnp.zeros((BLOCK, GROUP, TILE), F32)
    steps = CHANNELS // BLOCK

    def total(b, acc):
        return acc + part(b)

    center = jnp.sum(lax.fori_loop(0, steps, total, zero, unroll=2), axis=0) * (1.0 / CHANNELS)

    def squares(b, acc):
        shifted = part(b) - center[None]
        return acc + shifted * shifted

    spread = jnp.sum(lax.fori_loop(0, steps, squares, zero, unroll=2), axis=0) * (1.0 / CHANNELS)
    scale = lax.rsqrt(spread + 1e-05)

    def write(b, carry):
        for u in range(BLOCK):
            c = b * BLOCK + u
            target[pl.ds(pl.multiple_of(c * GROUP, GROUP), GROUP), :] = (
                (source[c, rows, :].astype(F32) - center) * scale * gain[c]
            )
        return carry

    lax.fori_loop(0, steps, write, 0, unroll=2)


def two_rows(source, p):
    first = source[pl.ds(2 * p, CHANNELS, stride=GROUP), :].astype(BF16)
    second = source[pl.ds(2 * p + 1, CHANNELS, stride=GROUP), :].astype(BF16)
    return jnp.concatenate([first, second], axis=1)


def put_rows(target, p, value):
    target[pl.ds(2 * p, OWN, stride=GROUP), :] = value[:, :TILE]
    target[pl.ds(2 * p + 1, OWN, stride=GROUP), :] = value[:, TILE:]


def pack(source, target, rows):
    def step(b, carry):
        block = source[pl.ds(pl.multiple_of(b * BLOCK * GROUP, GROUP), BLOCK * GROUP), :]
        target[pl.ds(b * BLOCK, BLOCK), rows, :] = block.reshape(BLOCK, GROUP, TILE).astype(BF16)
        return carry

    lax.fori_loop(0, OWN // BLOCK, step, 0, unroll=2)


def kernel(
    pair, mask_hbm, gain_in_hbm, gain_out_hbm, mask_rows_hbm, w_in_hbm, w_out_hbm, out,
    mask_s, gain_in, gain_out, mask_v, w_in, w_out, whole, normed, stage_a, stage_b, left, right, gate, lbuf, rbuf, rturn, pbuf, prod,
    own_x, xsend, xrecv, rsend, rrecv, lsend, lrecv, psend, precv, qsend, qrecv, own, fetched,
):
    h = lax.axis_index("chan")
    row, col = lax.axis_index("row"), lax.axis_index("col")
    me = row * 8 + col
    home = h * OWN
    partner = (1 - h) * OWN + me
    mine = pl.ds(home, OWN)
    cols = pl.ds(pl.multiple_of(col * TILE, TILE), TILE)

    def load(k):
        rows = pl.ds(*X_CHUNKS[k])
        return pltpu.make_async_copy(pair.at[:, rows, :], whole.at[mine, rows, :], own_x.at[k])

    def swap(k):
        rows = pl.ds(*X_CHUNKS[k])
        return pltpu.make_async_remote_copy(
            src_ref=pair.at[:, rows, :],
            dst_ref=whole.at[mine, rows, :],
            send_sem=xsend.at[k],
            recv_sem=xrecv.at[k],
            device_id=partner,
            device_id_type=LOGICAL,
        )

    barrier = pltpu.get_barrier_semaphore()
    greet(lambda t: pl.semaphore_signal(barrier, inc=1, device_id=home + t, device_id_type=LOGICAL))
    pl.semaphore_signal(barrier, inc=1, device_id=partner, device_id_type=LOGICAL)
    operands = (
        (mask_hbm, mask_s),
        (gain_in_hbm, gain_in),
        (gain_out_hbm, gain_out),
        (mask_rows_hbm, mask_v),
        (w_in_hbm, w_in),
        (w_out_hbm, w_out),
    )
    fetches = [pltpu.make_async_copy(src, dst, fetched.at[k]) for k, (src, dst) in enumerate(operands)]
    for k in range(len(X_CHUNKS)):
        load(k).start()
    for fetch in fetches:
        fetch.start()
    for fetch in fetches:
        fetch.wait()
    pl.semaphore_wait(barrier, 64)
    for k in range(len(X_CHUNKS)):
        swap(k).start()

    def scatter(source, rows, target, send_sem, recv_sem, own_sem):
        def send(t):
            pltpu.make_async_remote_copy(
                src_ref=source.at[t, rows, :],
                dst_ref=target,
                send_sem=send_sem,
                recv_sem=recv_sem,
                device_id=home + t,
                device_id_type=LOGICAL,
            ).start()

        peers(send)
        pltpu.make_async_copy(source.at[me, rows, :], target, own_sem).start()

    def others(send_sem, recv_sem, size):
        return pltpu.make_async_remote_copy(
            src_ref=left.at[pl.ds(0, 63), pl.ds(0, size), :],
            dst_ref=right.at[pl.ds(0, 63), pl.ds(0, size), :],
            send_sem=send_sem,
            recv_sem=recv_sem,
            device_id=partner,
            device_id_type=LOGICAL,
        )

    def right_target(first, size):
        return rbuf.at[aligned(row * TILE + first, size), cols]

    def left_target(first, size):
        return lbuf.at[aligned(first * 8 + row * size, size), cols]

    col_mask = mask_v[pl.ds(col, 1), :].astype(F32)

    def front(g, carry):
        for k, (start, _) in enumerate(X_CHUNKS):

            @pl.when(g * GROUP == start)
            def _():
                load(k).wait()
                swap(k).wait()

        first = g * GROUP
        rows = aligned(first, GROUP)
        layer_norm(whole, rows, gain_in, normed)
        for p in range(GROUP // 2):
            i = first + 2 * p
            proj = jnp.dot(w_in[...], two_rows(normed, p), preferred_element_type=F32)
            mask = jnp.concatenate([col_mask * mask_s[row * TILE + i + e].astype(F32) for e in range(2)], axis=1)
            put_rows(stage_a, p, sigmoid(proj[0:64]) * proj[64:128] * mask)
            put_rows(stage_b, p, sigmoid(proj[128:192]) * proj[192:256] * mask)
            opened = sigmoid(proj[256:320])
            gate[i] = opened[:, :TILE]
            gate[i + 1] = opened[:, TILE:]
        pack(stage_b, right, rows)
        pack(stage_a, left, rows)
        for k, (start, size) in enumerate(R_CHUNKS):

            @pl.when(first + GROUP == start + size)
            def _():
                scatter(right, pl.ds(start, size), right_target(start, size), rsend, rrecv, own.at[0, k])

        return carry

    lax.fori_loop(0, TILE // GROUP, front, 0)
    for k, (start, size) in enumerate(L_CHUNKS):
        scatter(left, pl.ds(start, size), left_target(start, size), lsend, lrecv.at[k], own.at[1, k])

    for k, (start, size) in enumerate(R_CHUNKS):
        pltpu.make_async_copy(right.at[me, pl.ds(start, size), :], right_target(start, size), own.at[0, k]).wait()
    others(rsend, rrecv, TILE).wait_recv()
    for b in range(8):
        rturn[:, b * TILE : b * TILE + TILE] = rbuf[b * TILE : b * TILE + TILE, :].T

    def product_slice(k, t):
        start, size = L_CHUNKS[k]
        return pbuf.at[t, pl.ds(start, size), :]

    def own_product(k):
        rows = pl.ds(*L_CHUNKS[k])
        return pltpu.make_async_copy(product_slice(k, me), prod.at[home + me, rows, :], own.at[2, k])

    def swap_product(k):
        rows = pl.ds(*L_CHUNKS[k])
        return pltpu.make_async_remote_copy(
            src_ref=prod.at[mine, rows, :],
            dst_ref=prod.at[mine, rows, :],
            send_sem=qsend.at[k],
            recv_sem=qrecv.at[k],
            device_id=partner,
            device_id_type=LOGICAL,
        )

    for k, (start, size) in enumerate(L_CHUNKS):
        pltpu.make_async_copy(left.at[me, pl.ds(start, size), :], left_target(start, size), own.at[1, k]).wait()
        others(lsend, lrecv.at[k], size).wait_recv()
        for half in range(2):
            tile = jnp.dot(
                lbuf[start * 8 : (start + size) * 8, :],
                rturn[:, half * 512 : half * 512 + 512],
                preferred_element_type=F32,
            ).astype(BF16)
            for r in range(8):
                for c in range(4):
                    pbuf[r * 8 + half * 4 + c, start : start + size, :] = tile[
                        r * size : r * size + size, c * TILE : c * TILE + TILE
                    ]
        rows = pl.ds(start, size)

        def send(t):
            pltpu.make_async_remote_copy(
                src_ref=product_slice(k, t),
                dst_ref=prod.at[home + me, rows, :],
                send_sem=psend,
                recv_sem=precv.at[k],
                device_id=home + t,
                device_id_type=LOGICAL,
            ).start()

        peers(send)
        own_product(k).start()

    def finish(first):
        rows = aligned(first, GROUP)
        layer_norm(prod, rows, gain_out, normed)
        for p in range(GROUP // 2):
            i = first + 2 * p
            mixed = jnp.dot(w_out[...], two_rows(normed, p), preferred_element_type=F32)
            put_rows(stage_a, p, mixed * jnp.concatenate([gate[i], gate[i + 1]], axis=1))
        pack(stage_a, out, rows)

    for k in range(len(L_CHUNKS) + 1):
        if k < len(L_CHUNKS):
            own_product(k).wait()
            others(psend, precv.at[k], L_CHUNKS[k][1]).wait_recv()
            swap_product(k).start()
        if k > 0:
            swap_product(k - 1).wait()
            start, size = L_CHUNKS[k - 1]

            def group(g, carry):
                finish(start + g * GROUP)
                return carry

            lax.fori_loop(0, size // GROUP, group, 0)
    others(rsend, rrecv, TILE).wait_send()
    others(lsend, rrecv, TILE).wait_send()
    others(psend, rrecv, TILE).wait_send()


def body(pair_acts, residue_mask, norm_in_gain, w_proj, norm_out_gain, w_out):
    vmem = pl.BlockSpec(memory_space=pltpu.VMEM)
    dma = pltpu.SemaphoreType.DMA
    parts = len(L_CHUNKS)
    return pl.pallas_call(
        kernel,
        out_shape=pltpu.VMEM((OWN, TILE, TILE), BF16),
        in_specs=[pl.BlockSpec(memory_space=pl.ANY)] * 7,
        out_specs=vmem,
        scratch_shapes=[
            pltpu.SMEM((8 * TILE,), jnp.int32),
            pltpu.SMEM((CHANNELS,), F32),
            pltpu.SMEM((CHANNELS,), F32),
            pltpu.VMEM((8, TILE), jnp.int32),
            pltpu.VMEM((5 * OWN, CHANNELS), BF16),
            pltpu.VMEM((OWN, CHANNELS), BF16),
            pltpu.VMEM((CHANNELS, TILE, TILE), BF16),
            pltpu.VMEM((CHANNELS * GROUP, TILE), F32),
            pltpu.VMEM((OWN * GROUP, TILE), F32),
            pltpu.VMEM((OWN * GROUP, TILE), F32),
            pltpu.VMEM((OWN, TILE, TILE), BF16),
            pltpu.VMEM((OWN, TILE, TILE), BF16),
            pltpu.VMEM((TILE, OWN, TILE), F32),
            pltpu.VMEM((8 * TILE, 8 * TILE), BF16),
            pltpu.VMEM((8 * TILE, 8 * TILE), BF16),
            pltpu.VMEM((8 * TILE, 8 * TILE), BF16),
            pltpu.VMEM((64, TILE, TILE), BF16),
            pltpu.VMEM((CHANNELS, TILE, TILE), BF16),
            dma((len(X_CHUNKS),)),
            dma((len(X_CHUNKS),)),
            dma((len(X_CHUNKS),)),
            dma,
            dma,
            dma,
            dma((parts,)),
            dma,
            dma((parts,)),
            dma((parts,)),
            dma((parts,)),
            dma((3, parts)),
            dma((6,)),
        ],
        compiler_params=pltpu.CompilerParams(collective_id=1, has_side_effects=True, vmem_limit_bytes=56 << 20),
        name="triangle",
    )(
        pair_acts,
        residue_mask,
        norm_in_gain,
        norm_out_gain,
        residue_mask.reshape(8, TILE),
        w_proj.reshape(5 * OWN, CHANNELS),
        w_out,
    )


def solution(mesh):
    return jax.shard_map(
        body,
        mesh=mesh,
        in_specs=(P("chan", "row", "col"), P(), P(), P(None, "chan", None), P(), P("chan", None)),
        out_specs=P("chan", "row", "col"),
        check_vma=False,
    )
```

```python
import jax
import jax.numpy as jnp
from jax import lax
from jax.experimental import pallas as pl
from jax.experimental.pallas import tpu as pltpu
from jax.sharding import PartitionSpec as P

LOGICAL = pl.DeviceIdType.LOGICAL
BF16 = jnp.bfloat16
F32 = jnp.float32
CHANNELS = 128
OWN = 64
TILE = 128
GROUP = 16
BLOCK = 8
X_CHUNKS = ((0, 16), (16, 48), (64, 64))
R_CHUNKS = ((0, 16), (16, 16), (32, 32), (64, 32), (96, 32))
L_CHUNKS = ((0, 32), (32, 32), (64, 32), (96, 16), (112, 16))
INNER = [(1, 2), (2, 1), (3, 3), (0, 1), (1, 0), (3, 2), (2, 3), (0, 2), (2, 0), (1, 1), (3, 1), (1, 3), (0, 3), (3, 0), (2, 2), (0, 0)]


def place():
    row, col = lax.axis_index("row"), lax.axis_index("col")
    return lax.axis_index("chan"), (row // 4) * 2 + col % 2, row % 4, col // 2


def peers(visit):
    _, x, y, z = place()
    along_y = [((y + d) % 4) * 8 for d in range(4)]
    along_z = [((z + d) % 4) * 2 for d in range(4)]

    def step(k, carry):
        d = (k + 1) % 4
        t = (x + d) % 4
        base = (t // 2) * 32 + t % 2
        for dy, dz in INNER[:15]:
            visit(base + along_y[dy] + along_z[dz])

        @pl.when(d != 0)
        def _():
            visit(base + along_y[0] + along_z[0])

        return carry

    lax.fori_loop(0, 4, step, 0)


def greet(visit):
    _, x, y, z = place()
    along_x = [(((x + d) % 4) // 2) * 32 + (x + d) % 2 for d in range(4)]
    along_y = [((y + d) % 4) * 8 for d in range(4)]
    along_z = [((z + d) % 4) * 2 for d in range(4)]
    offsets = [(a, b, c) for a in range(4) for b in range(4) for c in range(4)][1:]
    for a, b, c in sorted(offsets, key=lambda o: -sum(min(d, 4 - d) for d in o)):
        visit(along_x[a] + along_y[b] + along_z[c])


def aligned(start, size):
    return pl.ds(pl.multiple_of(start, GROUP), size)


def sigmoid(value):
    return 0.5 * jnp.tanh(0.5 * value) + 0.5


def layer_norm(source, rows, gain, target):
    def part(b):
        return source[pl.ds(b * BLOCK, BLOCK), rows, :].astype(F32)

    zero = jnp.zeros((BLOCK, GROUP, TILE), F32)
    steps = CHANNELS // BLOCK

    def total(b, acc):
        return acc + part(b)

    center = jnp.sum(lax.fori_loop(0, steps, total, zero, unroll=2), axis=0) * (1.0 / CHANNELS)

    def squares(b, acc):
        shifted = part(b) - center[None]
        return acc + shifted * shifted

    spread = jnp.sum(lax.fori_loop(0, steps, squares, zero, unroll=2), axis=0) * (1.0 / CHANNELS)
    scale = lax.rsqrt(spread + 1e-05)

    def write(b, carry):
        for u in range(BLOCK):
            c = b * BLOCK + u
            target[pl.ds(pl.multiple_of(c * GROUP, GROUP), GROUP), :] = (
                (source[c, rows, :].astype(F32) - center) * scale * gain[c]
            )
        return carry

    lax.fori_loop(0, steps, write, 0, unroll=2)


def two_rows(source, p):
    first = source[pl.ds(2 * p, CHANNELS, stride=GROUP), :].astype(BF16)
    second = source[pl.ds(2 * p + 1, CHANNELS, stride=GROUP), :].astype(BF16)
    return jnp.concatenate([first, second], axis=1)


def put_rows(target, p, value):
    target[pl.ds(2 * p, OWN, stride=GROUP), :] = value[:, :TILE]
    target[pl.ds(2 * p + 1, OWN, stride=GROUP), :] = value[:, TILE:]


def pack(source, target, rows):
    def step(b, carry):
        block = source[pl.ds(pl.multiple_of(b * BLOCK * GROUP, GROUP), BLOCK * GROUP), :]
        target[pl.ds(b * BLOCK, BLOCK), rows, :] = block.reshape(BLOCK, GROUP, TILE).astype(BF16)
        return carry

    lax.fori_loop(0, OWN // BLOCK, step, 0, unroll=2)


def kernel(
    pair, mask_hbm, gain_in_hbm, gain_out_hbm, mask_rows_hbm, w_in_hbm, w_out_hbm, out,
    mask_s, gain_in, gain_out, mask_v, w_in, w_out, whole, normed, stage_a, stage_b, left, right, gate, lbuf, rbuf, rturn, pbuf, prod,
    own_x, xsend, xrecv, rsend, rrecv, lsend, lrecv, psend, precv, qsend, qrecv, own, fetched, ready, go,
):
    h = lax.axis_index("chan")
    row, col = lax.axis_index("row"), lax.axis_index("col")
    me = row * 8 + col
    home = h * OWN
    partner = (1 - h) * OWN + me
    mine = pl.ds(home, OWN)
    cols = pl.ds(pl.multiple_of(col * TILE, TILE), TILE)

    def load(k):
        rows = pl.ds(*X_CHUNKS[k])
        return pltpu.make_async_copy(pair.at[:, rows, :], whole.at[mine, rows, :], own_x.at[k])

    def swap(k):
        rows = pl.ds(*X_CHUNKS[k])
        return pltpu.make_async_remote_copy(
            src_ref=pair.at[:, rows, :],
            dst_ref=whole.at[mine, rows, :],
            send_sem=xsend.at[k],
            recv_sem=xrecv.at[k],
            device_id=partner,
            device_id_type=LOGICAL,
        )

    barrier = pltpu.get_barrier_semaphore()

    @pl.when(h == 1)
    def _():
        pl.semaphore_signal(barrier, inc=1, device_id=partner, device_id_type=LOGICAL)

    greet(lambda t: pl.semaphore_signal(barrier, inc=1, device_id=OWN + t, device_id_type=LOGICAL))
    operands = (
        (mask_hbm, mask_s),
        (gain_in_hbm, gain_in),
        (gain_out_hbm, gain_out),
        (mask_rows_hbm, mask_v),
        (w_in_hbm, w_in),
        (w_out_hbm, w_out),
    )
    fetches = [pltpu.make_async_copy(src, dst, fetched.at[k]) for k, (src, dst) in enumerate(operands)]
    for k in range(len(X_CHUNKS)):
        load(k).start()
    for fetch in fetches:
        fetch.start()

    @pl.when(h == 0)
    def _():
        pl.semaphore_wait(barrier, 1)
        pl.semaphore_signal(ready, inc=1, device_id=partner, device_id_type=LOGICAL)

    @pl.when(h == 1)
    def _():
        pl.semaphore_wait(ready, 1)

    for k in range(len(X_CHUNKS)):
        swap(k).start()
    for fetch in fetches:
        fetch.wait()

    def all_here():
        @pl.when(h == 1)
        def _():
            pl.semaphore_wait(barrier, 126)
            pl.semaphore_signal(go, inc=1, device_id=partner, device_id_type=LOGICAL)

        @pl.when(h == 0)
        def _():
            pl.semaphore_wait(go, 1)

    def scatter(source, rows, target, send_sem, recv_sem, own_sem):
        def send(t):
            pltpu.make_async_remote_copy(
                src_ref=source.at[t, rows, :],
                dst_ref=target,
                send_sem=send_sem,
                recv_sem=recv_sem,
                device_id=home + t,
                device_id_type=LOGICAL,
            ).start()

        peers(send)
        pltpu.make_async_copy(source.at[me, rows, :], target, own_sem).start()

    def others(send_sem, recv_sem, size):
        return pltpu.make_async_remote_copy(
            src_ref=left.at[pl.ds(0, 63), pl.ds(0, size), :],
            dst_ref=right.at[pl.ds(0, 63), pl.ds(0, size), :],
            send_sem=send_sem,
            recv_sem=recv_sem,
            device_id=partner,
            device_id_type=LOGICAL,
        )

    def right_target(first, size):
        return rbuf.at[aligned(row * TILE + first, size), cols]

    def left_target(first, size):
        return lbuf.at[aligned(first * 8 + row * size, size), cols]

    col_mask = mask_v[pl.ds(col, 1), :].astype(F32)

    def front(g, carry):
        for k, (start, _) in enumerate(X_CHUNKS):

            @pl.when(g * GROUP == start)
            def _():
                load(k).wait()
                swap(k).wait()

        first = g * GROUP
        rows = aligned(first, GROUP)
        layer_norm(whole, rows, gain_in, normed)
        for p in range(GROUP // 2):
            i = first + 2 * p
            proj = jnp.dot(w_in[...], two_rows(normed, p), preferred_element_type=F32)
            mask = jnp.concatenate([col_mask * mask_s[row * TILE + i + e].astype(F32) for e in range(2)], axis=1)
            put_rows(stage_a, p, sigmoid(proj[0:64]) * proj[64:128] * mask)
            put_rows(stage_b, p, sigmoid(proj[128:192]) * proj[192:256] * mask)
            opened = sigmoid(proj[256:320])
            gate[i] = opened[:, :TILE]
            gate[i + 1] = opened[:, TILE:]
        pack(stage_b, right, rows)
        pack(stage_a, left, rows)

        @pl.when(g == 0)
        def _():
            all_here()

        for k, (start, size) in enumerate(R_CHUNKS):

            @pl.when(first + GROUP == start + size)
            def _():
                scatter(right, pl.ds(start, size), right_target(start, size), rsend, rrecv, own.at[0, k])

        return carry

    lax.fori_loop(0, TILE // GROUP, front, 0)
    for k, (start, size) in enumerate(L_CHUNKS):
        scatter(left, pl.ds(start, size), left_target(start, size), lsend, lrecv.at[k], own.at[1, k])

    for k, (start, size) in enumerate(R_CHUNKS):
        pltpu.make_async_copy(right.at[me, pl.ds(start, size), :], right_target(start, size), own.at[0, k]).wait()
    others(rsend, rrecv, TILE).wait_recv()
    for b in range(8):
        rturn[:, b * TILE : b * TILE + TILE] = rbuf[b * TILE : b * TILE + TILE, :].T

    def product_slice(k, t):
        start, size = L_CHUNKS[k]
        return pbuf.at[t, pl.ds(start, size), :]

    def own_product(k):
        rows = pl.ds(*L_CHUNKS[k])
        return pltpu.make_async_copy(product_slice(k, me), prod.at[home + me, rows, :], own.at[2, k])

    def swap_product(k):
        rows = pl.ds(*L_CHUNKS[k])
        return pltpu.make_async_remote_copy(
            src_ref=prod.at[mine, rows, :],
            dst_ref=prod.at[mine, rows, :],
            send_sem=qsend.at[k],
            recv_sem=qrecv.at[k],
            device_id=partner,
            device_id_type=LOGICAL,
        )

    for k, (start, size) in enumerate(L_CHUNKS):
        pltpu.make_async_copy(left.at[me, pl.ds(start, size), :], left_target(start, size), own.at[1, k]).wait()
        others(lsend, lrecv.at[k], size).wait_recv()
        for half in range(2):
            tile = jnp.dot(
                lbuf[start * 8 : (start + size) * 8, :],
                rturn[:, half * 512 : half * 512 + 512],
                preferred_element_type=F32,
            ).astype(BF16)
            for r in range(8):
                for c in range(4):
                    pbuf[r * 8 + half * 4 + c, start : start + size, :] = tile[
                        r * size : r * size + size, c * TILE : c * TILE + TILE
                    ]
        rows = pl.ds(start, size)

        def send(t):
            pltpu.make_async_remote_copy(
                src_ref=product_slice(k, t),
                dst_ref=prod.at[home + me, rows, :],
                send_sem=psend,
                recv_sem=precv.at[k],
                device_id=home + t,
                device_id_type=LOGICAL,
            ).start()

        peers(send)
        own_product(k).start()

    def finish(first):
        rows = aligned(first, GROUP)
        layer_norm(prod, rows, gain_out, normed)
        for p in range(GROUP // 2):
            i = first + 2 * p
            mixed = jnp.dot(w_out[...], two_rows(normed, p), preferred_element_type=F32)
            put_rows(stage_a, p, mixed * jnp.concatenate([gate[i], gate[i + 1]], axis=1))
        pack(stage_a, out, rows)

    for k in range(len(L_CHUNKS) + 1):
        if k < len(L_CHUNKS):
            own_product(k).wait()
            others(psend, precv.at[k], L_CHUNKS[k][1]).wait_recv()
            swap_product(k).start()
        if k > 0:
            swap_product(k - 1).wait()
            start, size = L_CHUNKS[k - 1]

            def group(g, carry):
                finish(start + g * GROUP)
                return carry

            lax.fori_loop(0, size // GROUP, group, 0)
    others(rsend, rrecv, TILE).wait_send()
    others(lsend, rrecv, TILE).wait_send()
    others(psend, rrecv, TILE).wait_send()


def body(pair_acts, residue_mask, norm_in_gain, w_proj, norm_out_gain, w_out):
    vmem = pl.BlockSpec(memory_space=pltpu.VMEM)
    dma = pltpu.SemaphoreType.DMA
    parts = len(L_CHUNKS)
    return pl.pallas_call(
        kernel,
        out_shape=pltpu.VMEM((OWN, TILE, TILE), BF16),
        in_specs=[pl.BlockSpec(memory_space=pl.ANY)] * 7,
        out_specs=vmem,
        scratch_shapes=[
            pltpu.SMEM((8 * TILE,), jnp.int32),
            pltpu.SMEM((CHANNELS,), F32),
            pltpu.SMEM((CHANNELS,), F32),
            pltpu.VMEM((8, TILE), jnp.int32),
            pltpu.VMEM((5 * OWN, CHANNELS), BF16),
            pltpu.VMEM((OWN, CHANNELS), BF16),
            pltpu.VMEM((CHANNELS, TILE, TILE), BF16),
            pltpu.VMEM((CHANNELS * GROUP, TILE), F32),
            pltpu.VMEM((OWN * GROUP, TILE), F32),
            pltpu.VMEM((OWN * GROUP, TILE), F32),
            pltpu.VMEM((OWN, TILE, TILE), BF16),
            pltpu.VMEM((OWN, TILE, TILE), BF16),
            pltpu.VMEM((TILE, OWN, TILE), F32),
            pltpu.VMEM((8 * TILE, 8 * TILE), BF16),
            pltpu.VMEM((8 * TILE, 8 * TILE), BF16),
            pltpu.VMEM((8 * TILE, 8 * TILE), BF16),
            pltpu.VMEM((64, TILE, TILE), BF16),
            pltpu.VMEM((CHANNELS, TILE, TILE), BF16),
            dma((len(X_CHUNKS),)),
            dma((len(X_CHUNKS),)),
            dma((len(X_CHUNKS),)),
            dma,
            dma,
            dma,
            dma((parts,)),
            dma,
            dma((parts,)),
            dma((parts,)),
            dma((parts,)),
            dma((3, parts)),
            dma((6,)),
            pltpu.SemaphoreType.REGULAR,
            pltpu.SemaphoreType.REGULAR,
        ],
        compiler_params=pltpu.CompilerParams(collective_id=1, has_side_effects=True, vmem_limit_bytes=56 << 20),
        name="triangle",
    )(
        pair_acts,
        residue_mask,
        norm_in_gain,
        norm_out_gain,
        residue_mask.reshape(8, TILE),
        w_proj.reshape(5 * OWN, CHANNELS),
        w_out,
    )


def solution(mesh):
    return jax.shard_map(
        body,
        mesh=mesh,
        in_specs=(P("chan", "row", "col"), P(), P(), P(None, "chan", None), P(), P("chan", None)),
        out_specs=P("chan", "row", "col"),
        check_vma=False,
    )
```

```python
import jax
import jax.numpy as jnp
from jax import lax
from jax.experimental import pallas as pl
from jax.experimental.pallas import tpu as pltpu
from jax.sharding import PartitionSpec as P

LOGICAL = pl.DeviceIdType.LOGICAL
BF16 = jnp.bfloat16
F32 = jnp.float32
CHANNELS = 128
OWN = 64
TILE = 128
GROUP = 16
BLOCK = 8
X_CHUNKS = ((0, 16), (16, 48), (64, 64))
R_CHUNKS = ((0, 16), (16, 16), (32, 16), (48, 16), (64, 32), (96, 32))
L_CHUNKS = ((0, 32), (32, 32), (64, 16), (80, 16), (96, 16), (112, 16))
INNER = [(1, 2), (2, 1), (3, 3), (0, 1), (1, 0), (3, 2), (2, 3), (0, 2), (2, 0), (1, 1), (3, 1), (1, 3), (0, 3), (3, 0), (2, 2), (0, 0)]


def place():
    row, col = lax.axis_index("row"), lax.axis_index("col")
    return lax.axis_index("chan"), (row // 4) * 2 + col % 2, row % 4, col // 2


def peers(visit):
    _, x, y, z = place()
    along_x = [(((x + d) % 4) // 2) * 32 + (x + d) % 2 for d in range(4)]
    along_y = [((y + d) % 4) * 8 for d in range(4)]

    def step(k, carry):
        d = (k + 1) % 4
        along_z = [((z + d + e) % 4) * 2 for e in range(4)]
        for dx, dy in INNER[:15]:
            visit(along_x[dx] + along_y[dy] + along_z[(8 - dx - dy) % 4])

        @pl.when(d != 0)
        def _():
            visit(along_x[0] + along_y[0] + along_z[0])

        return carry

    lax.fori_loop(0, 4, step, 0)


def greet(visit):
    _, x, y, z = place()
    along_x = [(((x + d) % 4) // 2) * 32 + (x + d) % 2 for d in range(4)]
    along_y = [((y + d) % 4) * 8 for d in range(4)]
    along_z = [((z + d) % 4) * 2 for d in range(4)]
    offsets = [(a, b, c) for a in range(4) for b in range(4) for c in range(4)][1:]
    for a, b, c in sorted(offsets, key=lambda o: -sum(min(d, 4 - d) for d in o)):
        visit(along_x[a] + along_y[b] + along_z[c])


def aligned(start, size):
    return pl.ds(pl.multiple_of(start, GROUP), size)


def sigmoid(value):
    return 0.5 * jnp.tanh(0.5 * value) + 0.5


def layer_norm(source, rows, gain, target):
    def part(b):
        return source[pl.ds(b * BLOCK, BLOCK), rows, :].astype(F32)

    zero = jnp.zeros((BLOCK, GROUP, TILE), F32)
    steps = CHANNELS // BLOCK

    def total(b, acc):
        return acc + part(b)

    center = jnp.sum(lax.fori_loop(0, steps, total, zero, unroll=2), axis=0) * (1.0 / CHANNELS)

    def squares(b, acc):
        shifted = part(b) - center[None]
        return acc + shifted * shifted

    spread = jnp.sum(lax.fori_loop(0, steps, squares, zero, unroll=2), axis=0) * (1.0 / CHANNELS)
    scale = lax.rsqrt(spread + 1e-05)

    def write(b, carry):
        for u in range(BLOCK):
            c = b * BLOCK + u
            target[pl.ds(pl.multiple_of(c * GROUP, GROUP), GROUP), :] = (
                (source[c, rows, :].astype(F32) - center) * scale * gain[c]
            )
        return carry

    lax.fori_loop(0, steps, write, 0, unroll=2)


def two_rows(source, p):
    first = source[pl.ds(2 * p, CHANNELS, stride=GROUP), :].astype(BF16)
    second = source[pl.ds(2 * p + 1, CHANNELS, stride=GROUP), :].astype(BF16)
    return jnp.concatenate([first, second], axis=1)


def put_rows(target, p, value):
    target[pl.ds(2 * p, OWN, stride=GROUP), :] = value[:, :TILE]
    target[pl.ds(2 * p + 1, OWN, stride=GROUP), :] = value[:, TILE:]


def pack(source, target, rows):
    def step(b, carry):
        block = source[pl.ds(pl.multiple_of(b * BLOCK * GROUP, GROUP), BLOCK * GROUP), :]
        target[pl.ds(b * BLOCK, BLOCK), rows, :] = block.reshape(BLOCK, GROUP, TILE).astype(BF16)
        return carry

    lax.fori_loop(0, OWN // BLOCK, step, 0, unroll=2)


def kernel(
    pair, mask_hbm, gain_in_hbm, gain_out_hbm, mask_rows_hbm, w_in_hbm, w_out_hbm, out,
    mask_s, gain_in, gain_out, mask_v, w_in, w_out, whole, normed, stage_a, stage_b, left, right, gate, lbuf, rbuf, rturn, pbuf, prod,
    own_x, xsend, xrecv, rsend, rrecv, lsend, lrecv, psend, precv, qsend, qrecv, own, fetched, ready, go,
):
    h = lax.axis_index("chan")
    row, col = lax.axis_index("row"), lax.axis_index("col")
    me = row * 8 + col
    home = h * OWN
    partner = (1 - h) * OWN + me
    mine = pl.ds(home, OWN)
    cols = pl.ds(pl.multiple_of(col * TILE, TILE), TILE)

    def load(k):
        rows = pl.ds(*X_CHUNKS[k])
        return pltpu.make_async_copy(pair.at[:, rows, :], whole.at[mine, rows, :], own_x.at[k])

    def swap(k):
        rows = pl.ds(*X_CHUNKS[k])
        return pltpu.make_async_remote_copy(
            src_ref=pair.at[:, rows, :],
            dst_ref=whole.at[mine, rows, :],
            send_sem=xsend.at[k],
            recv_sem=xrecv.at[k],
            device_id=partner,
            device_id_type=LOGICAL,
        )

    barrier = pltpu.get_barrier_semaphore()

    @pl.when(h == 1)
    def _():
        pl.semaphore_signal(barrier, inc=1, device_id=partner, device_id_type=LOGICAL)

    greet(lambda t: pl.semaphore_signal(barrier, inc=1, device_id=OWN + t, device_id_type=LOGICAL))
    operands = (
        (mask_hbm, mask_s),
        (gain_in_hbm, gain_in),
        (gain_out_hbm, gain_out),
        (mask_rows_hbm, mask_v),
        (w_in_hbm, w_in),
        (w_out_hbm, w_out),
    )
    fetches = [pltpu.make_async_copy(src, dst, fetched.at[k]) for k, (src, dst) in enumerate(operands)]
    for k in range(len(X_CHUNKS)):
        load(k).start()
    for fetch in fetches:
        fetch.start()

    @pl.when(h == 0)
    def _():
        pl.semaphore_wait(barrier, 1)
        pl.semaphore_signal(ready, inc=1, device_id=partner, device_id_type=LOGICAL)

    @pl.when(h == 1)
    def _():
        pl.semaphore_wait(ready, 1)

    for k in range(len(X_CHUNKS)):
        swap(k).start()
    for fetch in fetches:
        fetch.wait()

    def all_here():
        @pl.when(h == 1)
        def _():
            pl.semaphore_wait(barrier, 126)
            pl.semaphore_signal(go, inc=1, device_id=partner, device_id_type=LOGICAL)

        @pl.when(h == 0)
        def _():
            pl.semaphore_wait(go, 1)

    def scatter(source, rows, target, send_sem, recv_sem, own_sem):
        def send(t):
            pltpu.make_async_remote_copy(
                src_ref=source.at[t, rows, :],
                dst_ref=target,
                send_sem=send_sem,
                recv_sem=recv_sem,
                device_id=home + t,
                device_id_type=LOGICAL,
            ).start()

        peers(send)
        pltpu.make_async_copy(source.at[me, rows, :], target, own_sem).start()

    def others(send_sem, recv_sem, size):
        return pltpu.make_async_remote_copy(
            src_ref=left.at[pl.ds(0, 63), pl.ds(0, size), :],
            dst_ref=right.at[pl.ds(0, 63), pl.ds(0, size), :],
            send_sem=send_sem,
            recv_sem=recv_sem,
            device_id=partner,
            device_id_type=LOGICAL,
        )

    def right_target(first, size):
        return rbuf.at[aligned(row * TILE + first, size), cols]

    def left_target(first, size):
        return lbuf.at[aligned(first * 8 + row * size, size), cols]

    col_mask = mask_v[pl.ds(col, 1), :].astype(F32)

    def front(g, carry):
        for k, (start, _) in enumerate(X_CHUNKS):

            @pl.when(g * GROUP == start)
            def _():
                load(k).wait()
                swap(k).wait()

        first = g * GROUP
        rows = aligned(first, GROUP)
        layer_norm(whole, rows, gain_in, normed)
        for p in range(GROUP // 2):
            i = first + 2 * p
            proj = jnp.dot(w_in[...], two_rows(normed, p), preferred_element_type=F32)
            mask = jnp.concatenate([col_mask * mask_s[row * TILE + i + e].astype(F32) for e in range(2)], axis=1)
            put_rows(stage_a, p, sigmoid(proj[0:64]) * proj[64:128] * mask)
            put_rows(stage_b, p, sigmoid(proj[128:192]) * proj[192:256] * mask)
            opened = sigmoid(proj[256:320])
            gate[i] = opened[:, :TILE]
            gate[i + 1] = opened[:, TILE:]
        pack(stage_b, right, rows)
        pack(stage_a, left, rows)

        @pl.when(g == 0)
        def _():
            all_here()

        for k, (start, size) in enumerate(R_CHUNKS):

            @pl.when(first + GROUP == start + size)
            def _():
                scatter(right, pl.ds(start, size), right_target(start, size), rsend, rrecv, own.at[0, k])

        return carry

    lax.fori_loop(0, TILE // GROUP, front, 0)
    for k, (start, size) in enumerate(L_CHUNKS):
        scatter(left, pl.ds(start, size), left_target(start, size), lsend, lrecv.at[k], own.at[1, k])

    for k, (start, size) in enumerate(R_CHUNKS):
        pltpu.make_async_copy(right.at[me, pl.ds(start, size), :], right_target(start, size), own.at[0, k]).wait()
    others(rsend, rrecv, TILE).wait_recv()
    for b in range(8):
        rturn[:, b * TILE : b * TILE + TILE] = rbuf[b * TILE : b * TILE + TILE, :].T

    def product_slice(k, t):
        start, size = L_CHUNKS[k]
        return pbuf.at[t, pl.ds(start, size), :]

    def own_product(k):
        rows = pl.ds(*L_CHUNKS[k])
        return pltpu.make_async_copy(product_slice(k, me), prod.at[home + me, rows, :], own.at[2, k])

    def swap_product(k):
        rows = pl.ds(*L_CHUNKS[k])
        return pltpu.make_async_remote_copy(
            src_ref=prod.at[mine, rows, :],
            dst_ref=prod.at[mine, rows, :],
            send_sem=qsend.at[k],
            recv_sem=qrecv.at[k],
            device_id=partner,
            device_id_type=LOGICAL,
        )

    for k, (start, size) in enumerate(L_CHUNKS):
        pltpu.make_async_copy(left.at[me, pl.ds(start, size), :], left_target(start, size), own.at[1, k]).wait()
        others(lsend, lrecv.at[k], size).wait_recv()
        for half in range(2):
            tile = jnp.dot(
                lbuf[start * 8 : (start + size) * 8, :],
                rturn[:, half * 512 : half * 512 + 512],
                preferred_element_type=F32,
            ).astype(BF16)
            for r in range(8):
                for c in range(4):
                    pbuf[r * 8 + half * 4 + c, start : start + size, :] = tile[
                        r * size : r * size + size, c * TILE : c * TILE + TILE
                    ]
        rows = pl.ds(start, size)

        def send(t):
            pltpu.make_async_remote_copy(
                src_ref=product_slice(k, t),
                dst_ref=prod.at[home + me, rows, :],
                send_sem=psend,
                recv_sem=precv.at[k],
                device_id=home + t,
                device_id_type=LOGICAL,
            ).start()

        peers(send)
        own_product(k).start()

    def finish(first):
        rows = aligned(first, GROUP)
        layer_norm(prod, rows, gain_out, normed)
        for p in range(GROUP // 2):
            i = first + 2 * p
            mixed = jnp.dot(w_out[...], two_rows(normed, p), preferred_element_type=F32)
            put_rows(stage_a, p, mixed * jnp.concatenate([gate[i], gate[i + 1]], axis=1))
        pack(stage_a, out, rows)

    for k in range(len(L_CHUNKS) + 1):
        if k < len(L_CHUNKS):
            own_product(k).wait()
            others(psend, precv.at[k], L_CHUNKS[k][1]).wait_recv()
            swap_product(k).start()
        if k > 0:
            swap_product(k - 1).wait()
            start, size = L_CHUNKS[k - 1]

            def group(g, carry):
                finish(start + g * GROUP)
                return carry

            lax.fori_loop(0, size // GROUP, group, 0)
    others(rsend, rrecv, TILE).wait_send()
    others(lsend, rrecv, TILE).wait_send()
    others(psend, rrecv, TILE).wait_send()


def body(pair_acts, residue_mask, norm_in_gain, w_proj, norm_out_gain, w_out):
    vmem = pl.BlockSpec(memory_space=pltpu.VMEM)
    dma = pltpu.SemaphoreType.DMA
    parts = len(L_CHUNKS)
    return pl.pallas_call(
        kernel,
        out_shape=pltpu.VMEM((OWN, TILE, TILE), BF16),
        in_specs=[pl.BlockSpec(memory_space=pl.ANY)] * 7,
        out_specs=vmem,
        scratch_shapes=[
            pltpu.SMEM((8 * TILE,), jnp.int32),
            pltpu.SMEM((CHANNELS,), F32),
            pltpu.SMEM((CHANNELS,), F32),
            pltpu.VMEM((8, TILE), jnp.int32),
            pltpu.VMEM((5 * OWN, CHANNELS), BF16),
            pltpu.VMEM((OWN, CHANNELS), BF16),
            pltpu.VMEM((CHANNELS, TILE, TILE), BF16),
            pltpu.VMEM((CHANNELS * GROUP, TILE), F32),
            pltpu.VMEM((OWN * GROUP, TILE), F32),
            pltpu.VMEM((OWN * GROUP, TILE), F32),
            pltpu.VMEM((OWN, TILE, TILE), BF16),
            pltpu.VMEM((OWN, TILE, TILE), BF16),
            pltpu.VMEM((TILE, OWN, TILE), F32),
            pltpu.VMEM((8 * TILE, 8 * TILE), BF16),
            pltpu.VMEM((8 * TILE, 8 * TILE), BF16),
            pltpu.VMEM((8 * TILE, 8 * TILE), BF16),
            pltpu.VMEM((64, TILE, TILE), BF16),
            pltpu.VMEM((CHANNELS, TILE, TILE), BF16),
            dma((len(X_CHUNKS),)),
            dma((len(X_CHUNKS),)),
            dma((len(X_CHUNKS),)),
            dma,
            dma,
            dma,
            dma((parts,)),
            dma,
            dma((parts,)),
            dma((parts,)),
            dma((parts,)),
            dma((3, parts)),
            dma((6,)),
            pltpu.SemaphoreType.REGULAR,
            pltpu.SemaphoreType.REGULAR,
        ],
        compiler_params=pltpu.CompilerParams(collective_id=1, has_side_effects=True, vmem_limit_bytes=56 << 20),
        name="triangle",
    )(
        pair_acts,
        residue_mask,
        norm_in_gain,
        norm_out_gain,
        residue_mask.reshape(8, TILE),
        w_proj.reshape(5 * OWN, CHANNELS),
        w_out,
    )


def solution(mesh):
    return jax.shard_map(
        body,
        mesh=mesh,
        in_specs=(P("chan", "row", "col"), P(), P(), P(None, "chan", None), P(), P("chan", None)),
        out_specs=P("chan", "row", "col"),
        check_vma=False,
    )
```

```python
import jax
import jax.numpy as jnp
from jax import lax
from jax.experimental import pallas as pl
from jax.experimental.pallas import tpu as pltpu
from jax.sharding import PartitionSpec as P

LOGICAL = pl.DeviceIdType.LOGICAL
BF16 = jnp.bfloat16
F32 = jnp.float32
CHANNELS = 128
OWN = 64
TILE = 128
GROUP = 16
BLOCK = 8
X_CHUNKS = ((0, 16), (16, 48), (64, 64))
R_CHUNKS = ((0, 16), (16, 16), (32, 16), (48, 16), (64, 32), (96, 32))
L_CHUNKS = ((0, 32), (32, 32), (64, 16), (80, 16), (96, 16), (112, 16))
INNER = [(1, 2), (2, 1), (3, 3), (0, 1), (1, 0), (3, 2), (2, 3), (0, 2), (2, 0), (1, 1), (3, 1), (1, 3), (0, 3), (3, 0), (2, 2), (0, 0)]


def place():
    row, col = lax.axis_index("row"), lax.axis_index("col")
    return lax.axis_index("chan"), (row // 4) * 2 + col % 2, row % 4, col // 2


def peers(visit):
    _, x, y, z = place()
    along_x = [(((x + d) % 4) // 2) * 32 + (x + d) % 2 for d in range(4)]
    along_y = [((y + d) % 4) * 8 for d in range(4)]

    def step(k, carry):
        d = (k + 1) % 4
        along_z = [((z + d + e) % 4) * 2 for e in range(4)]
        for dx, dy in INNER[:15]:
            visit(along_x[dx] + along_y[dy] + along_z[(8 - dx - dy) % 4])

        @pl.when(d != 0)
        def _():
            visit(along_x[0] + along_y[0] + along_z[0])

        return carry

    lax.fori_loop(0, 4, step, 0)


def greet(visit):
    _, x, y, z = place()
    along_x = [(((x + d) % 4) // 2) * 32 + (x + d) % 2 for d in range(4)]
    along_y = [((y + d) % 4) * 8 for d in range(4)]
    along_z = [((z + d) % 4) * 2 for d in range(4)]
    offsets = [(a, b, c) for a in range(4) for b in range(4) for c in range(4)][1:]
    for a, b, c in sorted(offsets, key=lambda o: -sum(min(d, 4 - d) for d in o)):
        visit(along_x[a] + along_y[b] + along_z[c])


def aligned(start, size):
    return pl.ds(pl.multiple_of(start, GROUP), size)


def sigmoid(value):
    return 0.5 * jnp.tanh(0.5 * value) + 0.5


def layer_norm(source, rows, gain, target):
    def part(b):
        return source[pl.ds(b * BLOCK, BLOCK), rows, :].astype(F32)

    zero = jnp.zeros((BLOCK, GROUP, TILE), F32)
    steps = CHANNELS // BLOCK

    def total(b, acc):
        return acc + part(b)

    center = jnp.sum(lax.fori_loop(0, steps, total, zero, unroll=4), axis=0) * (1.0 / CHANNELS)

    def squares(b, acc):
        shifted = part(b) - center[None]
        return acc + shifted * shifted

    spread = jnp.sum(lax.fori_loop(0, steps, squares, zero, unroll=4), axis=0) * (1.0 / CHANNELS)
    scale = lax.rsqrt(spread + 1e-05)

    def write(b, carry):
        for u in range(BLOCK):
            c = b * BLOCK + u
            target[pl.ds(pl.multiple_of(c * GROUP, GROUP), GROUP), :] = (
                (source[c, rows, :].astype(F32) - center) * scale * gain[c]
            )
        return carry

    lax.fori_loop(0, steps, write, 0, unroll=4)


def two_rows(source, p):
    first = source[pl.ds(2 * p, CHANNELS, stride=GROUP), :].astype(BF16)
    second = source[pl.ds(2 * p + 1, CHANNELS, stride=GROUP), :].astype(BF16)
    return jnp.concatenate([first, second], axis=1)


def put_rows(target, p, value):
    target[pl.ds(2 * p, OWN, stride=GROUP), :] = value[:, :TILE]
    target[pl.ds(2 * p + 1, OWN, stride=GROUP), :] = value[:, TILE:]


def pack(source, target, rows):
    def step(b, carry):
        block = source[pl.ds(pl.multiple_of(b * BLOCK * GROUP, GROUP), BLOCK * GROUP), :]
        target[pl.ds(b * BLOCK, BLOCK), rows, :] = block.reshape(BLOCK, GROUP, TILE).astype(BF16)
        return carry

    lax.fori_loop(0, OWN // BLOCK, step, 0, unroll=2)


def kernel(
    pair, mask_hbm, gain_in_hbm, gain_out_hbm, mask_rows_hbm, w_in_hbm, w_out_hbm, out,
    mask_s, gain_in, gain_out, mask_v, w_in, w_out, whole, normed, stage_a, stage_b, left, right, gate, lbuf, rbuf, rturn, pbuf, prod,
    own_x, xsend, xrecv, rsend, rrecv, lsend, lrecv, psend, precv, qsend, qrecv, own, fetched, ready, go,
):
    h = lax.axis_index("chan")
    row, col = lax.axis_index("row"), lax.axis_index("col")
    me = row * 8 + col
    home = h * OWN
    partner = (1 - h) * OWN + me
    mine = pl.ds(home, OWN)
    cols = pl.ds(pl.multiple_of(col * TILE, TILE), TILE)

    def load(k):
        rows = pl.ds(*X_CHUNKS[k])
        return pltpu.make_async_copy(pair.at[:, rows, :], whole.at[mine, rows, :], own_x.at[k])

    def swap(k):
        rows = pl.ds(*X_CHUNKS[k])
        return pltpu.make_async_remote_copy(
            src_ref=pair.at[:, rows, :],
            dst_ref=whole.at[mine, rows, :],
            send_sem=xsend,
            recv_sem=xrecv.at[k],
            device_id=partner,
            device_id_type=LOGICAL,
        )

    barrier = pltpu.get_barrier_semaphore()

    @pl.when(h == 1)
    def _():
        pl.semaphore_signal(barrier, inc=1, device_id=partner, device_id_type=LOGICAL)

    greet(lambda t: pl.semaphore_signal(barrier, inc=1, device_id=OWN + t, device_id_type=LOGICAL))
    operands = (
        (mask_hbm, mask_s),
        (gain_in_hbm, gain_in),
        (gain_out_hbm, gain_out),
        (mask_rows_hbm, mask_v),
        (w_in_hbm, w_in),
        (w_out_hbm, w_out),
    )
    fetches = [pltpu.make_async_copy(src, dst, fetched.at[k]) for k, (src, dst) in enumerate(operands)]
    for k in range(len(X_CHUNKS)):
        load(k).start()
    for fetch in fetches:
        fetch.start()

    @pl.when(h == 0)
    def _():
        pl.semaphore_wait(barrier, 1)
        pl.semaphore_signal(ready, inc=1, device_id=partner, device_id_type=LOGICAL)

    @pl.when(h == 1)
    def _():
        pl.semaphore_wait(ready, 1)

    for k in range(len(X_CHUNKS)):
        swap(k).start()
    for fetch in fetches:
        fetch.wait()

    def all_here():
        @pl.when(h == 1)
        def _():
            pl.semaphore_wait(barrier, 126)
            pl.semaphore_signal(go, inc=1, device_id=partner, device_id_type=LOGICAL)

        @pl.when(h == 0)
        def _():
            pl.semaphore_wait(go, 1)

    def scatter(source, rows, target, send_sem, recv_sem, own_sem):
        def send(t):
            pltpu.make_async_remote_copy(
                src_ref=source.at[t, rows, :],
                dst_ref=target,
                send_sem=send_sem,
                recv_sem=recv_sem,
                device_id=home + t,
                device_id_type=LOGICAL,
            ).start()

        peers(send)
        pltpu.make_async_copy(source.at[me, rows, :], target, own_sem).start()

    def others(send_sem, recv_sem, size):
        return pltpu.make_async_remote_copy(
            src_ref=left.at[pl.ds(0, 63), pl.ds(0, size), :],
            dst_ref=right.at[pl.ds(0, 63), pl.ds(0, size), :],
            send_sem=send_sem,
            recv_sem=recv_sem,
            device_id=partner,
            device_id_type=LOGICAL,
        )

    def right_target(first, size):
        return rbuf.at[aligned(row * TILE + first, size), cols]

    def left_target(first, size):
        return lbuf.at[aligned(first * 8 + row * size, size), cols]

    col_mask = mask_v[pl.ds(col, 1), :].astype(F32)

    def front(g, carry):
        for k, (start, _) in enumerate(X_CHUNKS):

            @pl.when(g * GROUP == start)
            def _():
                load(k).wait()
                swap(k).wait_recv()

        first = g * GROUP
        rows = aligned(first, GROUP)
        layer_norm(whole, rows, gain_in, normed)
        for p in range(GROUP // 2):
            i = first + 2 * p
            proj = jnp.dot(w_in[...], two_rows(normed, p), preferred_element_type=F32)
            mask = jnp.concatenate([col_mask * mask_s[row * TILE + i + e].astype(F32) for e in range(2)], axis=1)
            put_rows(stage_a, p, sigmoid(proj[0:64]) * proj[64:128] * mask)
            put_rows(stage_b, p, sigmoid(proj[128:192]) * proj[192:256] * mask)
            opened = sigmoid(proj[256:320])
            gate[i] = opened[:, :TILE]
            gate[i + 1] = opened[:, TILE:]
        pack(stage_b, right, rows)
        pack(stage_a, left, rows)

        @pl.when(g == 0)
        def _():
            all_here()

        for k, (start, size) in enumerate(R_CHUNKS):

            @pl.when(first + GROUP == start + size)
            def _():
                scatter(right, pl.ds(start, size), right_target(start, size), rsend, rrecv, own.at[0])

        return carry

    lax.fori_loop(0, TILE // GROUP, front, 0)
    for k, (start, size) in enumerate(L_CHUNKS):
        scatter(left, pl.ds(start, size), left_target(start, size), lsend, lrecv.at[k], own.at[1])

    pltpu.make_async_copy(right.at[me], right_target(0, TILE), own.at[0]).wait()
    others(rsend, rrecv, TILE).wait_recv()
    pltpu.make_async_copy(left.at[me], right_target(0, TILE), own.at[1]).wait()
    for b in range(8):
        rturn[:, b * TILE : b * TILE + TILE] = rbuf[b * TILE : b * TILE + TILE, :].T

    def product_slice(k, t):
        start, size = L_CHUNKS[k]
        return pbuf.at[t, pl.ds(start, size), :]

    def own_product(k):
        rows = pl.ds(*L_CHUNKS[k])
        return pltpu.make_async_copy(product_slice(k, me), prod.at[home + me, rows, :], own.at[2])

    def swap_product(k):
        rows = pl.ds(*L_CHUNKS[k])
        return pltpu.make_async_remote_copy(
            src_ref=prod.at[mine, rows, :],
            dst_ref=prod.at[mine, rows, :],
            send_sem=qsend,
            recv_sem=qrecv.at[k],
            device_id=partner,
            device_id_type=LOGICAL,
        )

    for k, (start, size) in enumerate(L_CHUNKS):
        others(lsend, lrecv.at[k], size).wait_recv()
        for half in range(2):
            tile = jnp.dot(
                lbuf[start * 8 : (start + size) * 8, :],
                rturn[:, half * 512 : half * 512 + 512],
                preferred_element_type=F32,
            ).astype(BF16)
            for r in range(8):
                for c in range(4):
                    pbuf[r * 8 + half * 4 + c, start : start + size, :] = tile[
                        r * size : r * size + size, c * TILE : c * TILE + TILE
                    ]
        rows = pl.ds(start, size)

        def send(t):
            pltpu.make_async_remote_copy(
                src_ref=product_slice(k, t),
                dst_ref=prod.at[home + me, rows, :],
                send_sem=psend,
                recv_sem=precv.at[k],
                device_id=home + t,
                device_id_type=LOGICAL,
            ).start()

        peers(send)
        own_product(k).start()

    def finish(first):
        rows = aligned(first, GROUP)
        layer_norm(prod, rows, gain_out, normed)
        for p in range(GROUP // 2):
            i = first + 2 * p
            mixed = jnp.dot(w_out[...], two_rows(normed, p), preferred_element_type=F32)
            put_rows(stage_a, p, mixed * jnp.concatenate([gate[i], gate[i + 1]], axis=1))
        pack(stage_a, out, rows)

    pltpu.make_async_copy(pbuf.at[me], prod.at[home + me], own.at[2]).wait()
    for k in range(len(L_CHUNKS) + 1):
        if k < len(L_CHUNKS):
            others(psend, precv.at[k], L_CHUNKS[k][1]).wait_recv()
            swap_product(k).start()
        if k > 0:
            swap_product(k - 1).wait_recv()
            start, size = L_CHUNKS[k - 1]

            def group(g, carry):
                finish(start + g * GROUP)
                return carry

            lax.fori_loop(0, size // GROUP, group, 0)
    others(rsend, rrecv, TILE).wait_send()
    others(lsend, rrecv, TILE).wait_send()
    others(psend, rrecv, TILE).wait_send()
    pltpu.make_async_remote_copy(
        src_ref=prod.at[mine],
        dst_ref=prod.at[mine],
        send_sem=qsend,
        recv_sem=rrecv,
        device_id=partner,
        device_id_type=LOGICAL,
    ).wait_send()
    pltpu.make_async_remote_copy(
        src_ref=pair,
        dst_ref=whole.at[mine],
        send_sem=xsend,
        recv_sem=rrecv,
        device_id=partner,
        device_id_type=LOGICAL,
    ).wait_send()


def body(pair_acts, residue_mask, norm_in_gain, w_proj, norm_out_gain, w_out):
    vmem = pl.BlockSpec(memory_space=pltpu.VMEM)
    dma = pltpu.SemaphoreType.DMA
    parts = len(L_CHUNKS)
    return pl.pallas_call(
        kernel,
        out_shape=pltpu.VMEM((OWN, TILE, TILE), BF16),
        in_specs=[pl.BlockSpec(memory_space=pl.ANY)] * 7,
        out_specs=vmem,
        scratch_shapes=[
            pltpu.SMEM((8 * TILE,), jnp.int32),
            pltpu.SMEM((CHANNELS,), F32),
            pltpu.SMEM((CHANNELS,), F32),
            pltpu.VMEM((8, TILE), jnp.int32),
            pltpu.VMEM((5 * OWN, CHANNELS), BF16),
            pltpu.VMEM((OWN, CHANNELS), BF16),
            pltpu.VMEM((CHANNELS, TILE, TILE), BF16),
            pltpu.VMEM((CHANNELS * GROUP, TILE), F32),
            pltpu.VMEM((OWN * GROUP, TILE), F32),
            pltpu.VMEM((OWN * GROUP, TILE), F32),
            pltpu.VMEM((OWN, TILE, TILE), BF16),
            pltpu.VMEM((OWN, TILE, TILE), BF16),
            pltpu.VMEM((TILE, OWN, TILE), F32),
            pltpu.VMEM((8 * TILE, 8 * TILE), BF16),
            pltpu.VMEM((8 * TILE, 8 * TILE), BF16),
            pltpu.VMEM((8 * TILE, 8 * TILE), BF16),
            pltpu.VMEM((64, TILE, TILE), BF16),
            pltpu.VMEM((CHANNELS, TILE, TILE), BF16),
            dma((len(X_CHUNKS),)),
            dma,
            dma((len(X_CHUNKS),)),
            dma,
            dma,
            dma,
            dma((parts,)),
            dma,
            dma((parts,)),
            dma,
            dma((parts,)),
            dma((3,)),
            dma((6,)),
            pltpu.SemaphoreType.REGULAR,
            pltpu.SemaphoreType.REGULAR,
        ],
        compiler_params=pltpu.CompilerParams(collective_id=1, has_side_effects=True, vmem_limit_bytes=56 << 20),
        name="triangle",
    )(
        pair_acts,
        residue_mask,
        norm_in_gain,
        norm_out_gain,
        residue_mask.reshape(8, TILE),
        w_proj.reshape(5 * OWN, CHANNELS),
        w_out,
    )


def solution(mesh):
    return jax.shard_map(
        body,
        mesh=mesh,
        in_specs=(P("chan", "row", "col"), P(), P(), P(None, "chan", None), P(), P("chan", None)),
        out_specs=P("chan", "row", "col"),
        check_vma=False,
    )
```

```python
import jax
import jax.numpy as jnp
from jax import lax
from jax.experimental import pallas as pl
from jax.experimental.pallas import tpu as pltpu
from jax.sharding import PartitionSpec as P

LOGICAL = pl.DeviceIdType.LOGICAL
BF16 = jnp.bfloat16
F32 = jnp.float32
CHANNELS = 128
OWN = 64
TILE = 128
GROUP = 16
BLOCK = 8
X_CHUNKS = ((0, 16), (16, 48), (64, 64))
R_CHUNKS = ((0, 16), (16, 16), (32, 16), (48, 16), (64, 16), (80, 16), (96, 16), (112, 16))
L_CHUNKS = ((0, 32), (32, 32), (64, 16), (80, 16), (96, 16), (112, 16))
INNER = [(1, 2), (2, 1), (3, 3), (0, 1), (1, 0), (3, 2), (2, 3), (0, 2), (2, 0), (1, 1), (3, 1), (1, 3), (0, 3), (3, 0), (2, 2), (0, 0)]


def place():
    row, col = lax.axis_index("row"), lax.axis_index("col")
    return lax.axis_index("chan"), (row // 4) * 2 + col % 2, row % 4, col // 2


def peers(visit):
    _, x, y, z = place()
    along_x = [(((x + d) % 4) // 2) * 32 + (x + d) % 2 for d in range(4)]
    along_y = [((y + d) % 4) * 8 for d in range(4)]

    def step(k, carry):
        d = (k + 1) % 4
        along_z = [((z + d + e) % 4) * 2 for e in range(4)]
        for dx, dy in INNER[:15]:
            visit(along_x[dx] + along_y[dy] + along_z[(8 - dx - dy) % 4])

        @pl.when(d != 0)
        def _():
            visit(along_x[0] + along_y[0] + along_z[0])

        return carry

    lax.fori_loop(0, 4, step, 0)


def greet(visit):
    _, x, y, z = place()
    along_x = [(((x + d) % 4) // 2) * 32 + (x + d) % 2 for d in range(4)]
    along_y = [((y + d) % 4) * 8 for d in range(4)]
    along_z = [((z + d) % 4) * 2 for d in range(4)]
    offsets = [(a, b, c) for a in range(4) for b in range(4) for c in range(4)][1:]
    for a, b, c in sorted(offsets, key=lambda o: -sum(min(d, 4 - d) for d in o)):
        visit(along_x[a] + along_y[b] + along_z[c])


def aligned(start, size):
    return pl.ds(pl.multiple_of(start, GROUP), size)


def sigmoid(value):
    return 0.5 * jnp.tanh(0.5 * value) + 0.5


def layer_norm(source, rows, gain, target):
    def part(b):
        return source[pl.ds(b * BLOCK, BLOCK), rows, :].astype(F32)

    zero = jnp.zeros((BLOCK, GROUP, TILE), F32)
    steps = CHANNELS // BLOCK

    def total(b, acc):
        return acc + part(b)

    center = jnp.sum(lax.fori_loop(0, steps, total, zero, unroll=4), axis=0) * (1.0 / CHANNELS)

    def squares(b, acc):
        shifted = part(b) - center[None]
        return acc + shifted * shifted

    spread = jnp.sum(lax.fori_loop(0, steps, squares, zero, unroll=4), axis=0) * (1.0 / CHANNELS)
    scale = lax.rsqrt(spread + 1e-05)

    def write(b, carry):
        for u in range(BLOCK):
            c = b * BLOCK + u
            target[pl.ds(pl.multiple_of(c * GROUP, GROUP), GROUP), :] = (
                (source[c, rows, :].astype(F32) - center) * scale * gain[c]
            )
        return carry

    lax.fori_loop(0, steps, write, 0, unroll=4)


def two_rows(source, p):
    first = source[pl.ds(2 * p, CHANNELS, stride=GROUP), :].astype(BF16)
    second = source[pl.ds(2 * p + 1, CHANNELS, stride=GROUP), :].astype(BF16)
    return jnp.concatenate([first, second], axis=1)


def put_rows(target, p, value):
    target[pl.ds(2 * p, OWN, stride=GROUP), :] = value[:, :TILE]
    target[pl.ds(2 * p + 1, OWN, stride=GROUP), :] = value[:, TILE:]


def pack(source, target, rows):
    def step(b, carry):
        block = source[pl.ds(pl.multiple_of(b * BLOCK * GROUP, GROUP), BLOCK * GROUP), :]
        target[pl.ds(b * BLOCK, BLOCK), rows, :] = block.reshape(BLOCK, GROUP, TILE).astype(BF16)
        return carry

    lax.fori_loop(0, OWN // BLOCK, step, 0, unroll=2)


def kernel(
    pair, mask_hbm, gain_in_hbm, gain_out_hbm, mask_rows_hbm, w_in_hbm, w_out_hbm, out,
    mask_s, gain_in, gain_out, mask_v, w_in, w_out, whole, normed, stage_a, stage_b, left, right, gate, lbuf, rbuf, rturn, pbuf, prod,
    own_x, xsend, xrecv, rsend, rrecv, lsend, lrecv, psend, precv, qsend, qrecv, own, fetched, ready, go,
):
    h = lax.axis_index("chan")
    row, col = lax.axis_index("row"), lax.axis_index("col")
    me = row * 8 + col
    home = h * OWN
    partner = (1 - h) * OWN + me
    mine = pl.ds(home, OWN)
    cols = pl.ds(pl.multiple_of(col * TILE, TILE), TILE)

    def load(k):
        rows = pl.ds(*X_CHUNKS[k])
        return pltpu.make_async_copy(pair.at[:, rows, :], whole.at[mine, rows, :], own_x.at[k])

    def swap(k):
        rows = pl.ds(*X_CHUNKS[k])
        return pltpu.make_async_remote_copy(
            src_ref=pair.at[:, rows, :],
            dst_ref=whole.at[mine, rows, :],
            send_sem=xsend,
            recv_sem=xrecv.at[k],
            device_id=partner,
            device_id_type=LOGICAL,
        )

    barrier = pltpu.get_barrier_semaphore()

    @pl.when(h == 1)
    def _():
        pl.semaphore_signal(barrier, inc=1, device_id=partner, device_id_type=LOGICAL)

    greet(lambda t: pl.semaphore_signal(barrier, inc=1, device_id=OWN + t, device_id_type=LOGICAL))
    operands = (
        (mask_hbm, mask_s),
        (gain_in_hbm, gain_in),
        (gain_out_hbm, gain_out),
        (mask_rows_hbm, mask_v),
        (w_in_hbm, w_in),
        (w_out_hbm, w_out),
    )
    fetches = [pltpu.make_async_copy(src, dst, fetched.at[k]) for k, (src, dst) in enumerate(operands)]
    for k in range(len(X_CHUNKS)):
        load(k).start()
    for fetch in fetches:
        fetch.start()

    @pl.when(h == 0)
    def _():
        pl.semaphore_wait(barrier, 1)
        pl.semaphore_signal(ready, inc=1, device_id=partner, device_id_type=LOGICAL)

    @pl.when(h == 1)
    def _():
        pl.semaphore_wait(ready, 1)

    for k in range(len(X_CHUNKS)):
        swap(k).start()
    for fetch in fetches:
        fetch.wait()

    def all_here():
        @pl.when(h == 1)
        def _():
            pl.semaphore_wait(barrier, 126)
            pl.semaphore_signal(go, inc=1, device_id=partner, device_id_type=LOGICAL)

        @pl.when(h == 0)
        def _():
            pl.semaphore_wait(go, 1)

    def scatter(source, rows, target, send_sem, recv_sem, own_sem):
        def send(t):
            pltpu.make_async_remote_copy(
                src_ref=source.at[t, rows, :],
                dst_ref=target,
                send_sem=send_sem,
                recv_sem=recv_sem,
                device_id=home + t,
                device_id_type=LOGICAL,
            ).start()

        peers(send)
        pltpu.make_async_copy(source.at[me, rows, :], target, own_sem).start()

    def others(send_sem, recv_sem, size):
        return pltpu.make_async_remote_copy(
            src_ref=left.at[pl.ds(0, 63), pl.ds(0, size), :],
            dst_ref=right.at[pl.ds(0, 63), pl.ds(0, size), :],
            send_sem=send_sem,
            recv_sem=recv_sem,
            device_id=partner,
            device_id_type=LOGICAL,
        )

    def right_target(first, size):
        return rbuf.at[aligned(row * TILE + first, size), cols]

    def left_target(first, size):
        return lbuf.at[aligned(first * 8 + row * size, size), cols]

    col_mask = mask_v[pl.ds(col, 1), :].astype(F32)

    def front(g, carry):
        for k, (start, _) in enumerate(X_CHUNKS):

            @pl.when(g * GROUP == start)
            def _():
                load(k).wait()
                swap(k).wait_recv()

        first = g * GROUP
        rows = aligned(first, GROUP)
        layer_norm(whole, rows, gain_in, normed)
        for p in range(GROUP // 2):
            i = first + 2 * p
            proj = jnp.dot(w_in[...], two_rows(normed, p), preferred_element_type=F32)
            mask = jnp.concatenate([col_mask * mask_s[row * TILE + i + e].astype(F32) for e in range(2)], axis=1)
            put_rows(stage_a, p, sigmoid(proj[0:64]) * proj[64:128] * mask)
            put_rows(stage_b, p, sigmoid(proj[128:192]) * proj[192:256] * mask)
            opened = sigmoid(proj[256:320])
            gate[i] = opened[:, :TILE]
            gate[i + 1] = opened[:, TILE:]
        pack(stage_b, right, rows)
        pack(stage_a, left, rows)

        @pl.when(g == 0)
        def _():
            all_here()

        for k, (start, size) in enumerate(R_CHUNKS):

            @pl.when(first + GROUP == start + size)
            def _():
                scatter(right, pl.ds(start, size), right_target(start, size), rsend, rrecv, own.at[0])

        return carry

    lax.fori_loop(0, TILE // GROUP, front, 0)
    for k, (start, size) in enumerate(L_CHUNKS):
        scatter(left, pl.ds(start, size), left_target(start, size), lsend, lrecv.at[k], own.at[1])

    pltpu.make_async_copy(right.at[me], right_target(0, TILE), own.at[0]).wait()
    others(rsend, rrecv, TILE).wait_recv()
    pltpu.make_async_copy(left.at[me], right_target(0, TILE), own.at[1]).wait()
    for b in range(8):
        rturn[:, b * TILE : b * TILE + TILE] = rbuf[b * TILE : b * TILE + TILE, :].T

    def product_slice(k, t):
        start, size = L_CHUNKS[k]
        return pbuf.at[t, pl.ds(start, size), :]

    def own_product(k):
        rows = pl.ds(*L_CHUNKS[k])
        return pltpu.make_async_copy(product_slice(k, me), prod.at[home + me, rows, :], own.at[2])

    def swap_product(k):
        rows = pl.ds(*L_CHUNKS[k])
        return pltpu.make_async_remote_copy(
            src_ref=prod.at[mine, rows, :],
            dst_ref=prod.at[mine, rows, :],
            send_sem=qsend,
            recv_sem=qrecv.at[k],
            device_id=partner,
            device_id_type=LOGICAL,
        )

    for k, (start, size) in enumerate(L_CHUNKS):
        others(lsend, lrecv.at[k], size).wait_recv()
        for half in range(2):
            tile = jnp.dot(
                lbuf[start * 8 : (start + size) * 8, :],
                rturn[:, half * 512 : half * 512 + 512],
                preferred_element_type=F32,
            ).astype(BF16)
            for r in range(8):
                for c in range(4):
                    pbuf[r * 8 + half * 4 + c, start : start + size, :] = tile[
                        r * size : r * size + size, c * TILE : c * TILE + TILE
                    ]
        rows = pl.ds(start, size)

        def send(t):
            pltpu.make_async_remote_copy(
                src_ref=product_slice(k, t),
                dst_ref=prod.at[home + me, rows, :],
                send_sem=psend,
                recv_sem=precv.at[k],
                device_id=home + t,
                device_id_type=LOGICAL,
            ).start()

        peers(send)
        own_product(k).start()

    def finish(first):
        rows = aligned(first, GROUP)
        layer_norm(prod, rows, gain_out, normed)
        for p in range(GROUP // 2):
            i = first + 2 * p
            mixed = jnp.dot(w_out[...], two_rows(normed, p), preferred_element_type=F32)
            put_rows(stage_a, p, mixed * jnp.concatenate([gate[i], gate[i + 1]], axis=1))
        pack(stage_a, out, rows)

    pltpu.make_async_copy(pbuf.at[me], prod.at[home + me], own.at[2]).wait()
    for k in range(len(L_CHUNKS) + 1):
        if k < len(L_CHUNKS):
            others(psend, precv.at[k], L_CHUNKS[k][1]).wait_recv()
            swap_product(k).start()
        if k > 0:
            swap_product(k - 1).wait_recv()
            start, size = L_CHUNKS[k - 1]

            def group(g, carry):
                finish(start + g * GROUP)
                return carry

            lax.fori_loop(0, size // GROUP, group, 0)
    others(rsend, rrecv, TILE).wait_send()
    others(lsend, rrecv, TILE).wait_send()
    others(psend, rrecv, TILE).wait_send()
    pltpu.make_async_remote_copy(
        src_ref=prod.at[mine],
        dst_ref=prod.at[mine],
        send_sem=qsend,
        recv_sem=rrecv,
        device_id=partner,
        device_id_type=LOGICAL,
    ).wait_send()
    pltpu.make_async_remote_copy(
        src_ref=pair,
        dst_ref=whole.at[mine],
        send_sem=xsend,
        recv_sem=rrecv,
        device_id=partner,
        device_id_type=LOGICAL,
    ).wait_send()


def body(pair_acts, residue_mask, norm_in_gain, w_proj, norm_out_gain, w_out):
    vmem = pl.BlockSpec(memory_space=pltpu.VMEM)
    dma = pltpu.SemaphoreType.DMA
    parts = len(L_CHUNKS)
    return pl.pallas_call(
        kernel,
        out_shape=pltpu.VMEM((OWN, TILE, TILE), BF16),
        in_specs=[pl.BlockSpec(memory_space=pl.ANY)] * 7,
        out_specs=vmem,
        scratch_shapes=[
            pltpu.SMEM((8 * TILE,), jnp.int32),
            pltpu.SMEM((CHANNELS,), F32),
            pltpu.SMEM((CHANNELS,), F32),
            pltpu.VMEM((8, TILE), jnp.int32),
            pltpu.VMEM((5 * OWN, CHANNELS), BF16),
            pltpu.VMEM((OWN, CHANNELS), BF16),
            pltpu.VMEM((CHANNELS, TILE, TILE), BF16),
            pltpu.VMEM((CHANNELS * GROUP, TILE), F32),
            pltpu.VMEM((OWN * GROUP, TILE), F32),
            pltpu.VMEM((OWN * GROUP, TILE), F32),
            pltpu.VMEM((OWN, TILE, TILE), BF16),
            pltpu.VMEM((OWN, TILE, TILE), BF16),
            pltpu.VMEM((TILE, OWN, TILE), F32),
            pltpu.VMEM((8 * TILE, 8 * TILE), BF16),
            pltpu.VMEM((8 * TILE, 8 * TILE), BF16),
            pltpu.VMEM((8 * TILE, 8 * TILE), BF16),
            pltpu.VMEM((64, TILE, TILE), BF16),
            pltpu.VMEM((CHANNELS, TILE, TILE), BF16),
            dma((len(X_CHUNKS),)),
            dma,
            dma((len(X_CHUNKS),)),
            dma,
            dma,
            dma,
            dma((parts,)),
            dma,
            dma((parts,)),
            dma,
            dma((parts,)),
            dma((3,)),
            dma((6,)),
            pltpu.SemaphoreType.REGULAR,
            pltpu.SemaphoreType.REGULAR,
        ],
        compiler_params=pltpu.CompilerParams(collective_id=1, has_side_effects=True, vmem_limit_bytes=56 << 20),
        name="triangle",
    )(
        pair_acts,
        residue_mask,
        norm_in_gain,
        norm_out_gain,
        residue_mask.reshape(8, TILE),
        w_proj.reshape(5 * OWN, CHANNELS),
        w_out,
    )


def solution(mesh):
    return jax.shard_map(
        body,
        mesh=mesh,
        in_specs=(P("chan", "row", "col"), P(), P(), P(None, "chan", None), P(), P("chan", None)),
        out_specs=P("chan", "row", "col"),
        check_vma=False,
    )
```

```python
import jax
import jax.numpy as jnp
from jax import lax
from jax.experimental import pallas as pl
from jax.experimental.pallas import tpu as pltpu
from jax.sharding import PartitionSpec as P

LOGICAL = pl.DeviceIdType.LOGICAL
BF16 = jnp.bfloat16
F32 = jnp.float32
CHANNELS = 128
OWN = 64
TILE = 128
GROUP = 16
BLOCK = 8
X_CHUNKS = ((0, 16), (16, 48), (64, 64))
R_CHUNKS = ((0, 16), (16, 16), (32, 16), (48, 16), (64, 32), (96, 32))
L_CHUNKS = ((0, 32), (32, 32), (64, 16), (80, 16), (96, 16), (112, 16))
INNER = [(1, 2), (2, 1), (3, 3), (0, 1), (1, 0), (3, 2), (2, 3), (0, 2), (2, 0), (1, 1), (3, 1), (1, 3), (0, 3), (3, 0), (2, 2), (0, 0)]


def place():
    row, col = lax.axis_index("row"), lax.axis_index("col")
    return lax.axis_index("chan"), (row // 4) * 2 + col % 2, row % 4, col // 2


def peers(visit):
    _, x, y, z = place()
    along_x = [(((x + d) % 4) // 2) * 32 + (x + d) % 2 for d in range(4)]
    along_y = [((y + d) % 4) * 8 for d in range(4)]

    def step(k, carry):
        d = (k + 1) % 4
        along_z = [((z + d + e) % 4) * 2 for e in range(4)]
        for dx, dy in INNER[:15]:
            visit(along_x[dx] + along_y[dy] + along_z[(8 - dx - dy) % 4])

        @pl.when(d != 0)
        def _():
            visit(along_x[0] + along_y[0] + along_z[0])

        return carry

    lax.fori_loop(0, 4, step, 0)


def greet(visit):
    _, x, y, z = place()
    along_x = [(((x + d) % 4) // 2) * 32 + (x + d) % 2 for d in range(4)]
    along_y = [((y + d) % 4) * 8 for d in range(4)]
    along_z = [((z + d) % 4) * 2 for d in range(4)]
    offsets = [(a, b, c) for a in range(4) for b in range(4) for c in range(4)][1:]
    for a, b, c in sorted(offsets, key=lambda o: -sum(min(d, 4 - d) for d in o)):
        visit(along_x[a] + along_y[b] + along_z[c])


def aligned(start, size):
    return pl.ds(pl.multiple_of(start, GROUP), size)


def sigmoid(value):
    return 0.5 * jnp.tanh(0.5 * value) + 0.5


def layer_norm(source, rows, gain, target):
    def part(b):
        return source[pl.ds(b * BLOCK, BLOCK), rows, :].astype(F32)

    zero = jnp.zeros((BLOCK, GROUP, TILE), F32)
    steps = CHANNELS // BLOCK

    def total(b, acc):
        return acc + part(b)

    center = jnp.sum(lax.fori_loop(0, steps, total, zero, unroll=4), axis=0) * (1.0 / CHANNELS)

    def squares(b, acc):
        shifted = part(b) - center[None]
        return acc + shifted * shifted

    spread = jnp.sum(lax.fori_loop(0, steps, squares, zero, unroll=4), axis=0) * (1.0 / CHANNELS)
    scale = lax.rsqrt(spread + 1e-05)

    def write(b, carry):
        for u in range(BLOCK):
            c = b * BLOCK + u
            target[pl.ds(pl.multiple_of(c * GROUP, GROUP), GROUP), :] = (
                (source[c, rows, :].astype(F32) - center) * scale * gain[c]
            )
        return carry

    lax.fori_loop(0, steps, write, 0, unroll=4)


def two_rows(source, p):
    first = source[pl.ds(2 * p, CHANNELS, stride=GROUP), :].astype(BF16)
    second = source[pl.ds(2 * p + 1, CHANNELS, stride=GROUP), :].astype(BF16)
    return jnp.concatenate([first, second], axis=1)


def put_rows(target, p, value):
    target[pl.ds(2 * p, OWN, stride=GROUP), :] = value[:, :TILE]
    target[pl.ds(2 * p + 1, OWN, stride=GROUP), :] = value[:, TILE:]


def pack(source, target, rows):
    def step(b, carry):
        block = source[pl.ds(pl.multiple_of(b * BLOCK * GROUP, GROUP), BLOCK * GROUP), :]
        target[pl.ds(b * BLOCK, BLOCK), rows, :] = block.reshape(BLOCK, GROUP, TILE).astype(BF16)
        return carry

    lax.fori_loop(0, OWN // BLOCK, step, 0, unroll=2)


def kernel(
    pair, mask_hbm, gain_in_hbm, gain_out_hbm, mask_rows_hbm, w_in_hbm, w_out_hbm, out,
    mask_s, gain_in, gain_out, mask_v, w_in, w_out, whole, normed, stage_a, stage_b, left, right, gate, lbuf, rbuf, rturn, pbuf, prod,
    own_x, xsend, xrecv, rsend, rrecv, lsend, lrecv, psend, precv, qsend, qrecv, own, fetched, ready, go,
):
    h = lax.axis_index("chan")
    row, col = lax.axis_index("row"), lax.axis_index("col")
    me = row * 8 + col
    home = h * OWN
    partner = (1 - h) * OWN + me
    mine = pl.ds(home, OWN)
    cols = pl.ds(pl.multiple_of(col * TILE, TILE), TILE)

    def load(k):
        rows = pl.ds(*X_CHUNKS[k])
        return pltpu.make_async_copy(pair.at[:, rows, :], whole.at[mine, rows, :], own_x.at[k])

    def swap(k):
        rows = pl.ds(*X_CHUNKS[k])
        return pltpu.make_async_remote_copy(
            src_ref=pair.at[:, rows, :],
            dst_ref=whole.at[mine, rows, :],
            send_sem=xsend,
            recv_sem=xrecv.at[k],
            device_id=partner,
            device_id_type=LOGICAL,
        )

    barrier = pltpu.get_barrier_semaphore()

    @pl.when(h == 1)
    def _():
        pl.semaphore_signal(barrier, inc=1, device_id=partner, device_id_type=LOGICAL)

    greet(lambda t: pl.semaphore_signal(barrier, inc=1, device_id=OWN + t, device_id_type=LOGICAL))
    operands = (
        (mask_hbm, mask_s),
        (gain_in_hbm, gain_in),
        (gain_out_hbm, gain_out),
        (mask_rows_hbm, mask_v),
        (w_in_hbm, w_in),
        (w_out_hbm, w_out),
    )
    fetches = [pltpu.make_async_copy(src, dst, fetched.at[k]) for k, (src, dst) in enumerate(operands)]
    for k in range(len(X_CHUNKS)):
        load(k).start()
    for fetch in fetches:
        fetch.start()

    @pl.when(h == 0)
    def _():
        pl.semaphore_wait(barrier, 1)
        pl.semaphore_signal(ready, inc=1, device_id=partner, device_id_type=LOGICAL)

    @pl.when(h == 1)
    def _():
        pl.semaphore_wait(ready, 1)

    for k in range(len(X_CHUNKS)):
        swap(k).start()
    for fetch in fetches:
        fetch.wait()

    def all_here():
        @pl.when(h == 1)
        def _():
            pl.semaphore_wait(barrier, 126)
            pl.semaphore_signal(go, inc=1, device_id=partner, device_id_type=LOGICAL)

        @pl.when(h == 0)
        def _():
            pl.semaphore_wait(go, 1)

    def scatter(source, rows, target, send_sem, recv_sem, own_sem):
        def send(t):
            pltpu.make_async_remote_copy(
                src_ref=source.at[t, rows, :],
                dst_ref=target,
                send_sem=send_sem,
                recv_sem=recv_sem,
                device_id=home + t,
                device_id_type=LOGICAL,
            ).start()

        peers(send)
        pltpu.make_async_copy(source.at[me, rows, :], target, own_sem).start()

    def others(send_sem, recv_sem, size):
        return pltpu.make_async_remote_copy(
            src_ref=left.at[pl.ds(0, 63), pl.ds(0, size), :],
            dst_ref=right.at[pl.ds(0, 63), pl.ds(0, size), :],
            send_sem=send_sem,
            recv_sem=recv_sem,
            device_id=partner,
            device_id_type=LOGICAL,
        )

    def right_target(first, size):
        return rbuf.at[aligned(row * TILE + first, size), cols]

    def left_target(first, size):
        return lbuf.at[aligned(first * 8 + row * size, size), cols]

    col_mask = mask_v[pl.ds(col, 1), :].astype(F32)

    def front(g, carry):
        for k, (start, _) in enumerate(X_CHUNKS):

            @pl.when(g * GROUP == start)
            def _():
                load(k).wait()
                swap(k).wait_recv()

        first = g * GROUP
        rows = aligned(first, GROUP)
        layer_norm(whole, rows, gain_in, normed)
        for p in range(GROUP // 2):
            i = first + 2 * p
            proj = jnp.dot(w_in[...], two_rows(normed, p), preferred_element_type=F32)
            mask = jnp.concatenate([col_mask * mask_s[row * TILE + i + e].astype(F32) for e in range(2)], axis=1)
            put_rows(stage_a, p, sigmoid(proj[0:64]) * proj[64:128] * mask)
            put_rows(stage_b, p, sigmoid(proj[128:192]) * proj[192:256] * mask)
            opened = sigmoid(proj[256:320])
            gate[i] = opened[:, :TILE]
            gate[i + 1] = opened[:, TILE:]
        pack(stage_b, right, rows)
        pack(stage_a, left, rows)

        @pl.when(g == 0)
        def _():
            all_here()

        for k, (start, size) in enumerate(R_CHUNKS):

            @pl.when(first + GROUP == start + size)
            def _():
                scatter(right, pl.ds(start, size), right_target(start, size), rsend, rrecv, own.at[0])

        return carry

    lax.fori_loop(0, TILE // GROUP, front, 0)
    for k, (start, size) in enumerate(L_CHUNKS):
        scatter(left, pl.ds(start, size), left_target(start, size), lsend, lrecv.at[k], own.at[1])

    pltpu.make_async_copy(right.at[me], right_target(0, TILE), own.at[0]).wait()
    others(rsend, rrecv, TILE).wait_recv()
    pltpu.make_async_copy(left.at[me], right_target(0, TILE), own.at[1]).wait()
    for b in range(8):
        rturn[:, b * TILE : b * TILE + TILE] = rbuf[b * TILE : b * TILE + TILE, :].T

    def product_slice(k, t):
        start, size = L_CHUNKS[k]
        return pbuf.at[t, pl.ds(start, size), :]

    def own_product(k):
        rows = pl.ds(*L_CHUNKS[k])
        return pltpu.make_async_copy(product_slice(k, me), prod.at[home + me, rows, :], own.at[2])

    def swap_product(k):
        rows = pl.ds(*L_CHUNKS[k])
        return pltpu.make_async_remote_copy(
            src_ref=prod.at[mine, rows, :],
            dst_ref=prod.at[mine, rows, :],
            send_sem=qsend,
            recv_sem=qrecv.at[k],
            device_id=partner,
            device_id_type=LOGICAL,
        )

    for k, (start, size) in enumerate(L_CHUNKS):
        others(lsend, lrecv.at[k], size).wait_recv()
        for half in range(2):
            tile = jnp.dot(
                lbuf[start * 8 : (start + size) * 8, :],
                rturn[:, half * 512 : half * 512 + 512],
                preferred_element_type=F32,
            ).astype(BF16)
            for r in range(8):
                for c in range(4):
                    pbuf[r * 8 + half * 4 + c, start : start + size, :] = tile[
                        r * size : r * size + size, c * TILE : c * TILE + TILE
                    ]
        rows = pl.ds(start, size)

        def send(t):
            pltpu.make_async_remote_copy(
                src_ref=product_slice(k, t),
                dst_ref=prod.at[home + me, rows, :],
                send_sem=psend,
                recv_sem=precv.at[k],
                device_id=home + t,
                device_id_type=LOGICAL,
            ).start()

        peers(send)
        own_product(k).start()

    def finish(first):
        rows = aligned(first, GROUP)
        layer_norm(prod, rows, gain_out, normed)
        for p in range(GROUP // 2):
            i = first + 2 * p
            mixed = jnp.dot(w_out[...], two_rows(normed, p), preferred_element_type=F32)
            put_rows(stage_a, p, mixed * jnp.concatenate([gate[i], gate[i + 1]], axis=1))
        pack(stage_a, out, rows)

    pltpu.make_async_copy(pbuf.at[me], prod.at[home + me], own.at[2]).wait()
    for k in range(len(L_CHUNKS) + 1):
        if k < len(L_CHUNKS):
            others(psend, precv.at[k], L_CHUNKS[k][1]).wait_recv()
            swap_product(k).start()
        if k > 0:
            swap_product(k - 1).wait_recv()
            start, size = L_CHUNKS[k - 1]

            def group(g, carry):
                finish(start + g * GROUP)
                return carry

            lax.fori_loop(0, size // GROUP, group, 0)
    others(rsend, rrecv, TILE).wait_send()
    others(lsend, rrecv, TILE).wait_send()
    others(psend, rrecv, TILE).wait_send()
    pltpu.make_async_remote_copy(
        src_ref=prod.at[mine],
        dst_ref=prod.at[mine],
        send_sem=qsend,
        recv_sem=rrecv,
        device_id=partner,
        device_id_type=LOGICAL,
    ).wait_send()
    pltpu.make_async_remote_copy(
        src_ref=pair,
        dst_ref=whole.at[mine],
        send_sem=xsend,
        recv_sem=rrecv,
        device_id=partner,
        device_id_type=LOGICAL,
    ).wait_send()


STORES = 4


def store_kernel(result, out, sems):
    size = OWN // STORES
    copies = [
        pltpu.make_async_copy(result.at[pl.ds(k * size, size)], out.at[pl.ds(k * size, size)], sems.at[k])
        for k in range(STORES)
    ]
    for copy in copies:
        copy.start()
    for copy in copies:
        copy.wait()


def body(pair_acts, residue_mask, norm_in_gain, w_proj, norm_out_gain, w_out):
    vmem = pl.BlockSpec(memory_space=pltpu.VMEM)
    dma = pltpu.SemaphoreType.DMA
    parts = len(L_CHUNKS)
    result = pl.pallas_call(
        kernel,
        out_shape=pltpu.VMEM((OWN, TILE, TILE), BF16),
        in_specs=[pl.BlockSpec(memory_space=pl.ANY)] * 7,
        out_specs=vmem,
        scratch_shapes=[
            pltpu.SMEM((8 * TILE,), jnp.int32),
            pltpu.SMEM((CHANNELS,), F32),
            pltpu.SMEM((CHANNELS,), F32),
            pltpu.VMEM((8, TILE), jnp.int32),
            pltpu.VMEM((5 * OWN, CHANNELS), BF16),
            pltpu.VMEM((OWN, CHANNELS), BF16),
            pltpu.VMEM((CHANNELS, TILE, TILE), BF16),
            pltpu.VMEM((CHANNELS * GROUP, TILE), F32),
            pltpu.VMEM((OWN * GROUP, TILE), F32),
            pltpu.VMEM((OWN * GROUP, TILE), F32),
            pltpu.VMEM((OWN, TILE, TILE), BF16),
            pltpu.VMEM((OWN, TILE, TILE), BF16),
            pltpu.VMEM((TILE, OWN, TILE), F32),
            pltpu.VMEM((8 * TILE, 8 * TILE), BF16),
            pltpu.VMEM((8 * TILE, 8 * TILE), BF16),
            pltpu.VMEM((8 * TILE, 8 * TILE), BF16),
            pltpu.VMEM((64, TILE, TILE), BF16),
            pltpu.VMEM((CHANNELS, TILE, TILE), BF16),
            dma((len(X_CHUNKS),)),
            dma,
            dma((len(X_CHUNKS),)),
            dma,
            dma,
            dma,
            dma((parts,)),
            dma,
            dma((parts,)),
            dma,
            dma((parts,)),
            dma((3,)),
            dma((6,)),
            pltpu.SemaphoreType.REGULAR,
            pltpu.SemaphoreType.REGULAR,
        ],
        compiler_params=pltpu.CompilerParams(collective_id=1, has_side_effects=True, vmem_limit_bytes=56 << 20),
        name="triangle",
    )(
        pair_acts,
        residue_mask,
        norm_in_gain,
        norm_out_gain,
        residue_mask.reshape(8, TILE),
        w_proj.reshape(5 * OWN, CHANNELS),
        w_out,
    )
    return pl.pallas_call(
        store_kernel,
        out_shape=jax.ShapeDtypeStruct((OWN, TILE, TILE), BF16),
        in_specs=[vmem],
        out_specs=pl.BlockSpec(memory_space=pl.ANY),
        scratch_shapes=[dma((STORES,))],
        compiler_params=pltpu.CompilerParams(vmem_limit_bytes=8 << 20),
        name="store",
    )(result)


def solution(mesh):
    return jax.shard_map(
        body,
        mesh=mesh,
        in_specs=(P("chan", "row", "col"), P(), P(), P(None, "chan", None), P(), P("chan", None)),
        out_specs=P("chan", "row", "col"),
        check_vma=False,
    )
```
